32 devices in a mesh: seq: 16 (over z, y, x), head: 2 (over core).
Axes of the slice: x: 2, y: 2, z: 4, core: 2. Of those that a mesh axis runs over, the one named last changes fastest.
Arguments:
- tokens: bfloat16 [8192, 1280], P('seq'), may hold values from -40 to 40
- norm_gain: float32 [1280], replicated, may hold values from 0.1 to 1.9
- w_query: bfloat16 [1280, 1280], P(None, 'head'), may hold values from -1 to 1
- w_key: bfloat16 [1280, 1280], P(None, 'head'), may hold values from -1 to 1
- w_value: bfloat16 [1280, 1280], P(None, 'head'), may hold values from -0.15625 to 0.15625
- w_out: bfloat16 [1280, 1280], P('head'), may hold values from -0.15625 to 0.15625
- conv_in_w: bfloat16 [1280, 768], P(None, 'head'), may hold values from -0.15625 to 0.15625
- conv_gate_w: bfloat16 [1280, 768], P(None, 'head'), may hold values from -0.15625 to 0.15625
- conv_taps: bfloat16 [128, 768], P(None, 'head'), may hold values from -0.5 to 0.5
- conv_out_w: bfloat16 [768, 1280], P('head'), may hold values from -0.21875 to 0.21875
- chain_starts: int32 [12], replicated, may hold values from 0 to 7230, as said below
- block_lists: int32 [64, 4], P('seq'), may hold values from 0 to 63, as said below
- block_counts: int32 [64], P('seq'), may hold values from 0 to 4, as said below
Outputs:
- mixed: bfloat16 [8192, 1280], P(('seq', 'head'))
The draws below stay inside these ranges and needn't reach their ends.
Inputs may be any that keep to these rules, and one draw needn't show every extreme that they name: chain_starts[0] is 0 and the starts increase; consecutive starts differ by 260 or more, and the last chain, which ends at token 8191, also has 260 tokens or more. `block_lists`: A shard is a run of 512 tokens. Every entry of row q, also past its count, names a key block in a shard one, two or three shards before or after the shard of query block q, never in that shard itself; the entries of one row are distinct. All rows of one query shard together name at most one block of any shard two or three shards away. Entries of row q of block_lists at slots block_counts[q] and beyond are not used.
All inputs are finite; a program needn't handle non-finite values.
Results may differ from the reference program's by a relative error of at most 0.012.
Values may be sent and summed in bfloat16 or wider, within the bound.
No kernel may reach another device: no remote copies, remote signals or barrier semaphores. Data moves between devices by JAX's collectives and lax.ppermute only.
A program may use at most 128 MiB of HBM per device.

```python
import math
import jax
import jax.numpy as jnp
from jax import lax

D = 1280
H = 20
HD = 64
CW = 768
KTAP = 128
BLK = 128
HALF = 512
NB = 4
CHMEAN = 640
JIT = 190
TOK_DEV = 512
TOKENS = 8192
NCH = 12
NQB = 64


def draw_tokens(key, part):
    drawn = jax.random.normal(jax.random.fold_in(key, 1), (TOKENS, D), jnp.float32)
    drawn = jnp.clip(drawn, -6.0, 6.0)
    return drawn.astype(jnp.bfloat16)


def query_key_weight(key, which):
    own_part = jnp.clip(jax.random.normal(jax.random.fold_in(key, 40 + which), (D, H * HD), jnp.float32), -5.0, 5.0)
    result = own_part * (1.5 / math.sqrt(D))
    return jnp.clip(result, -1.0, 1.0).astype(jnp.bfloat16)


def draw_w_query(key, part):
    return query_key_weight(key, 0)


def draw_w_key(key, part):
    return query_key_weight(key, 1)


def draw_chain_starts(key, part):
    chain_ids = jnp.arange(NCH, dtype=jnp.int32)
    jitter = jax.random.randint(jax.random.fold_in(key, 60), (NCH,), -JIT, JIT + 1, dtype=jnp.int32)
    jitter = jnp.where(chain_ids == NCH - 1, JIT, jitter)
    return chain_ids * CHMEAN + jnp.where(chain_ids == 0, 0, jitter)


def list_tables(key):
    per_shard = TOK_DEV // BLK
    shard_total = TOKENS // TOK_DEV
    block_total = TOKENS // BLK
    shard_ids = jnp.arange(shard_total, dtype=jnp.int32)
    far_pick = jax.random.randint(jax.random.fold_in(key, 70), (shard_total, 4), 0, per_shard, dtype=jnp.int32)
    near_shift = jnp.concatenate([jnp.full((per_shard,), -1, jnp.int32), jnp.full((per_shard,), 1, jnp.int32)])
    far_shift = jnp.array([-3, -2, 2, 3], jnp.int32)
    cand_shard = jnp.concatenate([shard_ids[:, None] + near_shift[None, :], shard_ids[:, None] + far_shift[None, :]], axis=1)
    near_local = jnp.tile(jnp.arange(per_shard, dtype=jnp.int32), 2)
    cand_local = jnp.concatenate([jnp.broadcast_to(near_local[None, :], (shard_total, 2 * per_shard)), far_pick], axis=1)
    cand_block = cand_shard * per_shard + cand_local
    cand_valid = (cand_shard >= 0) & (cand_shard < shard_total)
    cand_width = 2 * per_shard + 4
    query_shard = jnp.arange(block_total, dtype=jnp.int32) // per_shard
    chosen = jax.random.randint(jax.random.fold_in(key, 71), (shard_total,), 0, per_shard, dtype=jnp.int32)
    forced = jnp.arange(block_total, dtype=jnp.int32) % per_shard == chosen[query_shard]
    target = jnp.where(query_shard + 2 < shard_total, 2 * per_shard + 2, 2 * per_shard + 1)
    column = jnp.arange(cand_width, dtype=jnp.int32)
    scores = jax.random.randint(jax.random.fold_in(key, 72), (block_total, cand_width), 0, 1 << 20, dtype=jnp.int32) * cand_width + column[None, :]
    scores = jnp.where(forced[:, None] & (column[None, :] == target[:, None]), (1 << 20) * cand_width + cand_width, scores)
    scores = jnp.where(cand_valid[query_shard], scores, -1 - column[None, :])
    ranking = jnp.argsort(-scores, axis=1)
    list_rows = jnp.take_along_axis(cand_block[query_shard], ranking[:, :NB], axis=1)
    counts = jax.random.randint(jax.random.fold_in(key, 73), (block_total,), 0, NB + 1, dtype=jnp.int32)
    counts = jnp.where(forced, NB, counts)
    return (list_rows.astype(jnp.int32), counts.astype(jnp.int32))


def draw_block_lists(key, part):
    return list_tables(key)[0]


def draw_block_counts(key, part):
    return list_tables(key)[1]


def block_levels(stream_key, dims, split, low, largest):
    def one(position, blocks):
        steps = jax.random.uniform(jax.random.fold_in(jax.random.fold_in(stream_key, 6), position), (blocks,), jnp.float32, low / len(split), largest / len(split))
        return jnp.repeat(jnp.exp(steps), dims[position] // blocks).reshape((-1,) + (1,) * (len(dims) - position - 1))

    level = one(*split[0])
    for cut in split[1:]:
        level = level * one(*cut)
    return level


def noise(rng, extent, width, most, split=(), kind=jnp.bfloat16):
    values = width * jax.random.normal(rng, extent, jnp.float32)
    if split:
        values = values * block_levels(rng, extent, split, -0.22, 0.18)
    return jnp.clip(values, -most, most).astype(kind)


def setup_inputs(seed: int = 0) -> dict:
    arg_keys = jax.random.split(jax.random.key(seed), 14)
    tokens = draw_tokens(jax.random.fold_in(arg_keys[13], 71), 0)
    norm_gain = jnp.clip(1.0 + 0.18 * jax.random.normal(arg_keys[1], (D,), jnp.float32), 0.1, 1.9)
    w_query = draw_w_query(jax.random.fold_in(arg_keys[13], 71), 0)
    w_key = draw_w_key(jax.random.fold_in(arg_keys[13], 71), 0)
    w_value = noise(arg_keys[4], (D, H * HD), D ** -0.5, 0.15625, ((1, 2),))
    w_out = noise(arg_keys[5], (H * HD, D), (H * HD) ** -0.5, 0.15625, ((0, 2),))
    conv_in_w = noise(arg_keys[6], (D, CW), D ** -0.5, 0.15625, ((1, 2),))
    conv_gate_w = noise(arg_keys[7], (D, CW), D ** -0.5, 0.15625, ((1, 2),))
    conv_taps = noise(arg_keys[8], (KTAP, CW), KTAP ** -0.5, 0.5, ((1, 2),))
    conv_out_w = noise(arg_keys[9], (CW, D), CW ** -0.5, 0.21875, ((0, 2),))
    chain_starts = draw_chain_starts(jax.random.fold_in(arg_keys[13], 71), 0)
    block_lists = draw_block_lists(jax.random.fold_in(arg_keys[13], 71), 0)
    block_counts = draw_block_counts(jax.random.fold_in(arg_keys[13], 71), 0)
    return dict(tokens=tokens, norm_gain=norm_gain, w_query=w_query, w_key=w_key, w_value=w_value, w_out=w_out, conv_in_w=conv_in_w, conv_gate_w=conv_gate_w, conv_taps=conv_taps, conv_out_w=conv_out_w, chain_starts=chain_starts, block_lists=block_lists, block_counts=block_counts)


def chain_index(positions, chain_starts):
    return lax.optimization_barrier(jnp.sum((chain_starts[None, :] <= positions[:, None]).astype(jnp.int32), axis=1)).astype(jnp.int32) - 1

def reference(tokens, norm_gain, w_query, w_key, w_value, w_out, conv_in_w, conv_gate_w, conv_taps, conv_out_w, chain_starts, block_lists, block_counts):
    inputs = tokens.astype(jnp.float32)
    normed = (inputs * lax.rsqrt(lax.optimization_barrier(jnp.mean(inputs * inputs, axis=1, keepdims=True)) + 1e-05) * norm_gain).astype(jnp.bfloat16)
    queries = jnp.dot(normed, w_query, preferred_element_type=jnp.float32).astype(jnp.bfloat16)
    key_rows = jnp.dot(normed, w_key, preferred_element_type=jnp.float32).astype(jnp.bfloat16)
    value_rows = jnp.dot(normed, w_value, preferred_element_type=jnp.float32).astype(jnp.bfloat16)
    positions = jnp.arange(TOKENS, dtype=jnp.int32)
    chain_of = chain_index(positions, chain_starts)
    key_pad = jnp.pad(key_rows, ((HALF, HALF), (0, 0)))
    value_pad = jnp.pad(value_rows, ((HALF, HALF), (0, 0)))
    chain_pad = jnp.pad(chain_of, (HALF, HALF), constant_values=-1)
    scale_factor = 1.0 / math.sqrt(HD)
    offsets = jnp.arange(BLK, dtype=jnp.int32)
    window_span = BLK + 2 * HALF

    def one_block(query_block):
        first_pos = (query_block * BLK).astype(jnp.int32)
        q_rows = lax.dynamic_slice_in_dim(queries, first_pos, BLK, 0)
        q_pos = first_pos + offsets
        q_chain = lax.dynamic_slice_in_dim(chain_of, first_pos, BLK, 0)
        near_keys = lax.dynamic_slice_in_dim(key_pad, first_pos, window_span, 0)
        near_values = lax.dynamic_slice_in_dim(value_pad, first_pos, window_span, 0)
        near_chain = lax.dynamic_slice_in_dim(chain_pad, first_pos, window_span, 0)
        near_pos = first_pos - HALF + jnp.arange(window_span, dtype=jnp.int32)
        relative = near_pos[None, :] - q_pos[:, None]
        near_mask = (relative >= -HALF) & (relative < HALF) & (near_chain[None, :] == q_chain[:, None])
        near_mask = near_mask & (near_pos[None, :] >= 0) & (near_pos[None, :] < TOKENS)
        picked = block_lists[query_block]
        list_pos = (picked[:, None] * BLK + offsets[None, :]).reshape(NB * BLK).astype(jnp.int32)
        list_keys = key_rows[list_pos]
        list_values = value_rows[list_pos]
        list_chain = chain_of[list_pos]
        slot_index = jnp.repeat(jnp.arange(NB, dtype=jnp.int32), BLK)
        list_mask = (slot_index[None, :] < block_counts[query_block]) & (list_chain[None, :] != q_chain[:, None])
        all_keys = jnp.concatenate([near_keys, list_keys], axis=0).astype(jnp.float32).reshape(window_span + NB * BLK, H, HD)
        all_values = jnp.concatenate([near_values, list_values], axis=0).astype(jnp.float32).reshape(window_span + NB * BLK, H, HD)
        all_mask = jnp.concatenate([near_mask, list_mask], axis=1)
        scores = jnp.einsum('qhd,khd->hqk', q_rows.astype(jnp.float32).reshape(BLK, H, HD), all_keys) * scale_factor
        scores = jnp.where(all_mask[None], scores, -jnp.inf)
        row_max = lax.optimization_barrier(jnp.max(scores, axis=2, keepdims=True))
        weights = jnp.where(all_mask[None], jnp.exp(scores - row_max), 0.0)
        probs = (weights / lax.optimization_barrier(jnp.sum(weights, axis=2, keepdims=True))).astype(jnp.bfloat16)
        mixed_heads = jnp.einsum('hqk,khd->qhd', probs.astype(jnp.float32), all_values)
        return mixed_heads.reshape(BLK, H * HD).astype(jnp.bfloat16)
    attended = lax.map(one_block, jnp.arange(NQB, dtype=jnp.int32)).reshape(TOKENS, H * HD)
    conv_input = jnp.dot(normed, conv_in_w, preferred_element_type=jnp.float32).astype(jnp.bfloat16)
    conv_gate = jnp.dot(normed, conv_gate_w, preferred_element_type=jnp.float32).astype(jnp.bfloat16)
    start_of = chain_starts[chain_of]
    padded = jnp.pad(conv_input.astype(jnp.float32), ((KTAP, 0), (0, 0)))
    tap_rows = conv_taps.astype(jnp.float32)

    def add_tap(tap_lag, running):
        tap_lag = jnp.asarray(tap_lag).astype(jnp.int32)
        shifted = lax.dynamic_slice_in_dim(padded, (KTAP - tap_lag).astype(jnp.int32), TOKENS, 0)
        weight_row = lax.dynamic_slice_in_dim(tap_rows, tap_lag, 1, 0)
        keep_mask = positions - tap_lag >= start_of
        return running + jnp.where(keep_mask[:, None], shifted * weight_row, 0.0)
    conv_sum = lax.fori_loop(0, KTAP, add_tap, jnp.zeros((TOKENS, CW), jnp.float32))
    gated = (conv_sum * jax.nn.silu(conv_gate.astype(jnp.float32))).astype(jnp.bfloat16)
    mixed = jnp.dot(attended, w_out, preferred_element_type=jnp.float32) + jnp.dot(gated, conv_out_w, preferred_element_type=jnp.float32)
    return mixed.astype(jnp.bfloat16)
```

```python
import functools
import math

import jax
import jax.numpy as jnp
from jax import lax
from jax.experimental import pallas as pl
from jax.experimental.pallas import tpu as pltpu
from jax.sharding import PartitionSpec as P


HD = 64
KTAP = 128
BLK = 128
HALF = 512
NB = 4
LANES = 128
AXES = ("seq", "head")
NEG = -1e30
F32 = jnp.float32
BF16 = jnp.bfloat16


def flat_pairs(count, target):
    pairs = []
    for i in range(count):
        for h in range(2):
            j = target(i, h)
            if 0 <= j < count:
                pairs.append((2 * i + h, 2 * j + h))
    return pairs


def swap(value):
    return lax.ppermute(value, "head", [(0, 1), (1, 0)])


def dot(a, b):
    return jnp.dot(a, b, preferred_element_type=F32)


SMEM = pl.BlockSpec(memory_space=pltpu.SMEM)
VMEM = pl.BlockSpec(memory_space=pltpu.VMEM)
ANY = pl.BlockSpec(memory_space=pl.ANY)


def limit(mib):
    return pltpu.CompilerParams(vmem_limit_bytes=mib << 20)


def in_hbm(value):
    return pltpu.with_memory_space_constraint(value, pltpu.HBM)


PIECES = 4


def plan_kernel(per_shard, nweights, lists_in, tokens, gain_in, *refs):
    weights, refs = refs[:nweights], refs[nweights:]
    mine, yours, normed, half, *refs = refs
    kept, (lists, gain, rows, sem) = refs[:nweights], refs[nweights:]
    me, core = lax.axis_index("seq"), lax.axis_index("head")
    size = tokens.shape[0] // PIECES
    copies = [
        pltpu.make_async_copy(
            tokens.at[pl.ds(n * size, size)], rows.at[pl.ds(n * size, size)], sem.at[n]
        )
        for n in range(PIECES)
    ]
    copies.append(pltpu.make_async_copy(lists_in, lists, sem.at[PIECES]))
    copies.append(pltpu.make_async_copy(gain_in, gain, sem.at[PIECES + 1]))
    for n in range(nweights):
        copies.append(pltpu.make_async_copy(weights[n], kept[n], sem.at[PIECES + 2 + n]))
    for copy in copies:
        copy.start()
    copies[PIECES + 1].wait()
    g = jnp.broadcast_to(gain[...].reshape(1, -1), (32, normed.shape[1]))

    def norm(r, c):
        here = pl.ds(pl.multiple_of(r * 32, 32), 32)
        x = rows[here, :].astype(F32)
        x = x * lax.rsqrt(jnp.mean(x * x, axis=1, keepdims=True) + 1e-05) * g
        normed[here, :] = x.astype(BF16)
        return c

    for n in range(PIECES):
        copies[n].wait()
        lax.fori_loop(n * size // 32, (n + 1) * size // 32, norm, 0)
    copies[PIECES].wait()

    def wanted(distance):
        low = (me + distance) * per_shard
        found = jnp.int32(0)
        for q in range(per_shard):
            for m in range(NB):
                local = lists[q, m] - low
                found = jnp.where((local >= 0) & (local < per_shard), local, found)
        return found

    side = 1 - 2 * core
    for n in range(2):
        mine[n] = wanted(side * (n + 2))
        yours[n] = wanted(-side * (n + 2))
    count = half.shape[0]
    half[...] = normed[pl.ds(pl.multiple_of(core * count, count), count), :]
    for copy in copies[PIECES + 2 :]:
        copy.wait()


def plan(lists, tokens, gain, weights):
    rows, cols = tokens.shape
    pair = jax.ShapeDtypeStruct((2,), jnp.int32)
    return pl.pallas_call(
        functools.partial(plan_kernel, rows // BLK, len(weights)),
        out_shape=[
            pair,
            pair,
            jax.ShapeDtypeStruct((rows, cols), BF16),
            jax.ShapeDtypeStruct((rows // 2, cols), BF16),
        ]
        + [jax.ShapeDtypeStruct(w.shape, BF16) for w in weights],
        in_specs=[ANY] * (3 + len(weights)),
        out_specs=[SMEM, SMEM] + [VMEM] * (2 + len(weights)),
        scratch_shapes=[
            pltpu.SMEM(lists.shape, jnp.int32),
            pltpu.VMEM(gain.shape, F32),
            pltpu.VMEM((rows, cols), BF16),
            pltpu.SemaphoreType.DMA((PIECES + 2 + len(weights),)),
        ],
        compiler_params=limit(14),
        name="plan",
    )(in_hbm(lists), in_hbm(tokens), in_hbm(gain), *[in_hbm(w) for w in weights])


def pick_own_kernel(asked, own, out):
    out[...] = own[pl.ds(pl.multiple_of(asked[0] * BLK, BLK), BLK), :]


def pick_other_kernel(asked, *refs):
    *parts, out = refs
    me, core = lax.axis_index("seq"), lax.axis_index("head")
    count = len(parts) // 2
    blocks = parts[0].shape[0] // BLK
    use_partner = (me % 2) == core
    slot = (asked[1] + core * (count * blocks // 2)) % (count * blocks)
    held = slot // blocks + jnp.where(use_partner, 0, count)
    here = pl.ds(pl.multiple_of((slot % blocks) * BLK, BLK), BLK)
    for k, ref in enumerate(parts):

        @pl.when(held == k)
        def _(ref=ref):
            out[...] = ref[here, :]


def pick(asked, sources):
    if len(sources) == 1:
        kernel = pick_own_kernel
    else:
        kernel = pick_other_kernel
    return pl.pallas_call(
        kernel,
        out_shape=jax.ShapeDtypeStruct((BLK, sources[0].shape[1]), BF16),
        in_specs=[SMEM] + [VMEM] * len(sources),
        out_specs=VMEM,
        compiler_params=limit(6),
        name="pick",
    )(asked, *sources)


def rim_rows(parts):
    mine, swapped = parts[len(parts) // 2 - 1], parts[-1]
    last = slice(mine.shape[0] - KTAP, mine.shape[0])
    return jnp.where(lax.axis_index("head") == 1, mine[last, :], swapped[last, :])


def own_kernel(scales, x_ref, *refs):
    count = len(scales)
    weights, outs = refs[:count], refs[count:]
    for n in range(count):
        y = dot(x_ref[...], weights[n][...])
        outs[n][...] = (y if scales[n] == 1.0 else y * scales[n]).astype(BF16)


def own_project(x, weights, scales):
    rows, cols = x.shape
    outs = [jax.ShapeDtypeStruct((rows, w.shape[1]), BF16) for w in weights]
    flops = sum(2 * rows * cols * w.shape[1] for w in weights)
    return pl.pallas_call(
        functools.partial(own_kernel, scales),
        out_shape=outs,
        in_specs=[VMEM] * (1 + len(weights)),
        out_specs=[VMEM] * len(outs),
        compiler_params=limit(14),
        cost_estimate=pl.CostEstimate(
            flops=flops, bytes_accessed=sum(w.size * 2 for w in weights), transcendentals=0
        ),
        name="own_project",
    )(x, *weights)


def other_kernel(*refs):
    *parts, wk, wv, wc, k_ref, v_ref, rim_ref = refs
    x = jnp.concatenate([part[...] for part in parts], axis=0)
    k_ref[...] = dot(x, wk[...]).astype(BF16)
    v_ref[...] = dot(x, wv[...]).astype(BF16)
    rim_ref[...] = dot(rim_rows(parts), wc[...]).astype(BF16)


def other_project(parts, wk, wv, wc):
    rows, cols = sum(part.shape[0] for part in parts), parts[0].shape[1]
    return pl.pallas_call(
        other_kernel,
        out_shape=[
            jax.ShapeDtypeStruct((rows, wk.shape[1]), BF16),
            jax.ShapeDtypeStruct((rows, wv.shape[1]), BF16),
            jax.ShapeDtypeStruct((KTAP, wc.shape[1]), BF16),
        ],
        in_specs=[VMEM] * (3 + len(parts)),
        out_specs=[VMEM] * 3,
        compiler_params=limit(10),
        cost_estimate=pl.CostEstimate(
            flops=4 * rows * cols * wk.shape[1], bytes_accessed=4 * wk.size, transcendentals=0
        ),
        name="other_project",
    )(*parts, wk, wv, wc)


BIG = 1 << 30
FAR = 1 << 20


def attention_kernel(
    first,
    fresh_parts,
    nch,
    per_shard,
    kblocks,
    starts,
    lists,
    counts,
    mine,
    yours,
    q_ref,
    *refs,
):
    k_in, v_in, *refs = refs
    new, (wk, wv, *refs) = refs[:fresh_parts], refs[fresh_parts:]
    if first:
        wc_in, o_ref, l_ref, mx_ref, rim_ref, *refs = refs
    else:
        o_ref, l_ref, mx_ref, g_ref, wo, wco, theirs, ours, *refs = refs
    k_all, v_all, qz, s_buf, bias, k_chain, i_chain, gblk, flag, ids, *refs = refs
    a_ref = None if first else refs[0]
    pairs = q_ref.shape[1] // LANES
    held = k_in.shape[0]
    k_all[:held] = k_in[...]
    v_all[:held] = v_in[...]
    fresh = jnp.concatenate([part[...] for part in new], axis=0)
    k_all[held:] = dot(fresh, wk[...]).astype(BF16)
    v_all[held:] = dot(fresh, wv[...]).astype(BF16)
    if first:
        rim_ref[...] = dot(rim_rows(new), wc_in[...]).astype(BF16)

    me, core = lax.axis_index("seq"), lax.axis_index("head")
    shards = lax.axis_size("seq")
    step = 1 - 2 * (me % 2)
    side = 1 - 2 * core
    turn = core * (per_shard // 2)
    own = me * per_shard

    def block_of(shard, local):
        return jnp.where((shard >= 0) & (shard < shards), shard * per_shard + local, -FAR)

    for p in range(per_shard):
        local = (turn + p) % per_shard
        if first:
            gblk[p] = own + p
            gblk[per_shard + p] = block_of(me + step, local)
        else:
            gblk[p] = block_of(me - step, local)
    if not first:
        for n in range(2):
            gblk[per_shard + 2 * n] = block_of(me + side * (n + 2), mine[n])
            gblk[per_shard + 2 * n + 1] = block_of(me - side * (n + 2), yours[n])

    def slot_of(block):
        shard = block // per_shard
        away = shard - me
        near_slot = (block % per_shard - turn) % per_shard
        if first:
            return jnp.where(away == step, per_shard + near_slot, kblocks)
        far_slot = per_shard + 2 * (jnp.abs(away) - 2) + jnp.where(away * side > 0, 0, 1)
        return jnp.where(
            away == -step, near_slot, jnp.where(jnp.abs(away) >= 2, far_slot, kblocks)
        )

    def chain_of(pos):
        return lax.fori_loop(
            0,
            nch,
            lambda c, n: n + jnp.where(starts[c] <= pos, 1, 0),
            jnp.full(pos.shape, -1, jnp.int32),
        )

    lane = lax.broadcasted_iota(jnp.int32, (BLK, LANES), 1)
    row = lax.broadcasted_iota(jnp.int32, (BLK, LANES), 0)
    low = lane < HD
    for b in range(kblocks):
        k_chain[pl.ds(b, 1), :] = gblk[b] * BLK + lane[0:1, :]
    k_chain[...] = chain_of(k_chain[...])
    bias[kblocks] = jnp.full((BLK, LANES), NEG, F32)

    def one_block(qb, carry):
        gq = own + qb
        q_first = gq * BLK
        q_last = q_first + BLK - 1

        def scan(c, found):
            begin, end, after = found
            s = starts[c]
            begin = jnp.where(s <= q_first, jnp.maximum(begin, s), begin)
            end = jnp.where(s > q_first, jnp.minimum(end, s), end)
            after = jnp.where(s > q_last, jnp.minimum(after, s), after)
            return begin, end, after

        begin, end, after = lax.fori_loop(
            0, nch, scan, (jnp.int32(0), jnp.int32(BIG), jnp.int32(BIG))
        )
        i_chain[...] = chain_of(q_first + row)
        zero = jnp.zeros((BLK, LANES), BF16)
        q_rows = pl.ds(pl.multiple_of(qb * BLK, BLK), BLK)
        for p in range(pairs):
            q = q_ref[q_rows, p * LANES : (p + 1) * LANES]
            qz[p, 0:BLK, :] = jnp.where(low, q, zero)
            qz[p, BLK : 2 * BLK, :] = jnp.where(low, zero, q)

        for b in range(kblocks + 1):
            flag[b] = 0

        def mark(m, c):
            flag[slot_of(lists[qb, m])] = 1
            return c

        lax.fori_loop(0, counts[qb], mark, 0)

        count = jnp.int32(0)
        for b in range(kblocks):
            gk = gblk[b]
            k_first = gk * BLK
            k_last = k_first + BLK - 1
            away = gk - gq
            near = (jnp.abs(away) * BLK <= HALF) & (k_last >= begin) & (k_first < after)
            listed = flag[b]
            one_chain = (k_first >= begin) & (jnp.maximum(k_last, q_last) < end)
            active = near | ((listed == 1) & jnp.logical_not(one_chain))
            ids[count] = b
            count = count + active.astype(jnp.int32)
            same = i_chain[...] == k_chain[b : b + 1, :]
            relative = away * BLK + lane - row
            in_window = jnp.where((relative >= -HALF) & (relative < HALF), 0.0, NEG)
            in_list = jnp.where(listed == 1, 0.0, NEG)
            bias[b] = jnp.where(same, in_window, in_list)
        ids[count] = kblocks
        ids[count + 1] = kblocks
        steps = jnp.maximum((count + 1) // 2, 1)

        def attend(steps):
            masks = [bias[ids[n]] for n in range(2 * steps)]
            rows_of = [
                pl.ds(pl.multiple_of(jnp.minimum(ids[n], kblocks - 1) * BLK, BLK), BLK)
                for n in range(2 * steps)
            ]
            for p in range(pairs):
                cols = slice(p * LANES, (p + 1) * LANES)
                if first:
                    m = None
                else:
                    old = mx_ref[q_rows, cols]
                    turned = pltpu.roll(old, HD, 1)
                    m = jnp.concatenate([jnp.where(low, old, turned), jnp.where(low, turned, old)], 0)
                for n in range(steps):
                    k = jnp.concatenate(
                        [k_all[rows_of[2 * n], cols], k_all[rows_of[2 * n + 1], cols]], axis=0
                    )
                    s = lax.dot_general(
                        qz[p], k, (((1,), (1,)), ((), ())), preferred_element_type=F32
                    )
                    mask = jnp.concatenate([masks[2 * n], masks[2 * n + 1]], axis=1)
                    s = s + jnp.concatenate([mask, mask], axis=0)
                    s_buf[p, n] = s
                    top = jnp.maximum(s[:, :LANES], s[:, LANES:])
                    m = top if m is None else jnp.maximum(m, top)
                m = jnp.broadcast_to(jnp.max(m, axis=1, keepdims=True), (2 * BLK, LANES))
                m2 = jnp.concatenate([m, m], axis=1)
                e = jnp.concatenate(
                    [jnp.exp2(s_buf[p, n] - m2).astype(BF16) for n in range(steps)], axis=1
                )
                v = jnp.concatenate([v_all[here, cols] for here in rows_of], axis=0)
                v = jnp.concatenate([v, jnp.ones_like(v)], axis=1)
                y = dot(e, v)
                o = jnp.where(low, y[:BLK, :LANES], y[BLK:, :LANES])
                l = jnp.where(low, y[:BLK, LANES:], y[BLK:, LANES:])
                m = jnp.where(low, m[:BLK], m[BLK:])
                if first:
                    o_ref[q_rows, cols] = o
                    l_ref[q_rows, cols] = l
                    mx_ref[q_rows, cols] = m
                else:
                    scale = jnp.exp2(old - m)
                    o = o + o_ref[q_rows, cols] * scale
                    l = l + l_ref[q_rows, cols] * scale
                    a_ref[q_rows, cols] = (o / l).astype(BF16)

        for n in range(1, kblocks // 2 + 1):

            @pl.when(steps == n)
            def _(n=n):
                attend(n)

        return carry

    lax.fori_loop(0, per_shard, one_block, 0)
    if not first:
        rows = ours.shape[0]
        for half, out in ((1 - core, theirs), (core, ours)):
            here = pl.ds(pl.multiple_of(half * rows, rows), rows)
            y = dot(a_ref[here, :], wo[...]) + dot(g_ref[here, :], wco[...])
            out[...] = y.astype(out.dtype)


def attention(context, queries, kv, new, weights, finish=None):
    rows, cols = queries.shape
    pairs = cols // LANES
    fresh = sum(part.shape[0] for part in new)
    keys = kv[0].shape[0] + fresh
    kblocks = keys // BLK
    steps = (kblocks + 1) // 2
    first = finish is None
    sums = jax.ShapeDtypeStruct((rows, cols), F32)
    if first:
        extra, more = (), []
        out_shape = [sums] * 3 + [jax.ShapeDtypeStruct((KTAP, weights[2].shape[1]), BF16)]
    else:
        extra, more = finish, [pltpu.VMEM((rows, cols), BF16)]
        wide = finish[4].shape[1]
        out_shape = [jax.ShapeDtypeStruct((rows // 2, wide), t) for t in (BF16, F32)]
    operands = (queries, *kv, *new, *weights, *extra)
    return pl.pallas_call(
        functools.partial(
            attention_kernel, first, len(new), context[0].shape[0], rows // BLK, kblocks
        ),
        out_shape=out_shape,
        in_specs=[SMEM] * len(context) + [VMEM] * len(operands),
        out_specs=[VMEM] * len(out_shape),
        scratch_shapes=[pltpu.VMEM((keys, cols), BF16)] * 2
        + [
            pltpu.VMEM((pairs, 2 * BLK, LANES), BF16),
            pltpu.VMEM((pairs, steps, 2 * BLK, 2 * BLK), F32),
            pltpu.VMEM((kblocks + 1, BLK, LANES), F32),
            pltpu.VMEM((kblocks, LANES), jnp.int32),
            pltpu.VMEM((BLK, LANES), jnp.int32),
            pltpu.SMEM((kblocks,), jnp.int32),
            pltpu.SMEM((kblocks + 1,), jnp.int32),
            pltpu.SMEM((kblocks + 2,), jnp.int32),
        ]
        + more,
        compiler_params=limit(32),
        cost_estimate=pl.CostEstimate(
            flops=4 * rows * keys * cols, bytes_accessed=4 * keys * cols, transcendentals=rows * keys
        ),
        name="attention",
    )(*context, *operands)


SEG = 8
KT = 8
JT = 16


def accumulate(accs, xv, wv):
    accs, taps = list(accs), len(wv)
    for n in range(taps):
        for j in range(len(accs)):
            accs[j] = accs[j] + xv[j - n + taps - 1] * wv[n]
    return tuple(accs)


def conv_kernel(
    nch, starts, own_ref, rim_p, rim_o, taps_ref, gate_ref, out_ref, x_ref, xs, ws, ms, y, x2, w2, y2
):
    rows, cols = own_ref.shape
    span = rows // SEG
    tiles = cols // LANES
    quarter, outs = KTAP // 4, span // 4
    me = lax.axis_index("seq")
    first = me * rows

    seg = lax.broadcasted_iota(jnp.int32, (SEG, LANES), 0)
    seg_first = first + seg * span

    def latest(c, found):
        begin, low = found
        s = starts[c]
        begin = jnp.where(s < seg_first + span, jnp.maximum(begin, s), begin)
        at = lax.rem(jnp.maximum(s - first, 0), span)
        inside = (s > first) & (s < first + rows) & (at > 0)
        return begin, jnp.where(inside, jnp.minimum(low, at), low)

    begin, low = lax.fori_loop(
        0, nch, latest, (jnp.zeros((SEG, LANES), jnp.int32), jnp.int32(span))
    )
    begin = begin - seg_first
    inner = begin > 0
    outer_begin = jnp.where(inner, -(1 << 30), begin)

    for t in range(tiles):
        cols_t = slice(t * LANES, (t + 1) * LANES)
        x_ref[t, 0:KTAP, :] = jnp.where(me % 2 == 1, rim_p[:, cols_t], rim_o[:, cols_t]).astype(F32)
        x_ref[t, pl.ds(KTAP, rows), :] = own_ref[:, cols_t].astype(F32)

    def row_of(j, t):
        v = x_ref[t, pl.ds(KTAP + j, SEG, stride=span), :]
        return jnp.where(j >= outer_begin, v, 0.0)

    def spread(n, before):
        j = 4 * (n - (quarter - 1))
        after = []
        for t in range(tiles):
            cols_t = slice(t * LANES, (t + 1) * LANES)
            a3, a2, a1 = before[3 * t : 3 * t + 3]
            b0, b1, b2, b3 = (row_of(j + k, t) for k in range(4))
            for s, (early, here, late) in enumerate(
                ((a1 - a2, b1 - b0, b3 - b2), (a2, b0, b2), (a2 - a3, b0 - a1, b2 - b1))
            ):
                xs[3 * s, n, :, cols_t] = late - here
                xs[3 * s + 1, n, :, cols_t] = here
                xs[3 * s + 2, n, :, cols_t] = here - early
            after += [b1, b2, b3]
        return tuple(after)

    start = 4 * (1 - quarter)
    lax.fori_loop(
        0,
        quarter - 1 + outs,
        spread,
        tuple(row_of(start + k, t) for t in range(tiles) for k in (-3, -2, -1)),
    )

    def widen(g, c):
        w = taps_ref[pl.ds(pl.multiple_of(g * 16, 16), 16), :].astype(F32)
        for r in range(4):
            w0, w1, w2, w3 = (w[4 * r + k : 4 * r + k + 1, :] for k in range(4))
            for s, (u, v) in enumerate(((w0, w2), (w0 + w1, w2 + w3), (w1, w3))):
                for k, value in enumerate((u, u + v, v)):
                    ws[3 * s + k, 4 * g + r] = jnp.broadcast_to(value, (SEG, cols))
        return c

    lax.fori_loop(0, KTAP // 16, widen, 0)

    for t in range(tiles):
        cols_t = slice(t * LANES, (t + 1) * LANES)

        def filtered(f, c, cols_t=cols_t):
            accs = tuple(jnp.zeros((SEG, LANES), F32) for _ in range(outs))
            for k0 in range(0, quarter, KT):
                at = quarter - k0 - KT
                xv = [xs[f, at + n, :, cols_t] for n in range(outs + KT - 1)]
                wv = [ws[f, k0 + n, :, cols_t] for n in range(KT)]
                accs = accumulate(accs, xv, wv)
            for j in range(outs):
                ms[f, j] = accs[j]
            return c

        lax.fori_loop(0, 9, filtered, 0)

        def join(b, c, cols_t=cols_t):
            odd, even = [], []
            for s in range(3):
                m0, m1, m2 = (ms[3 * s + k, b] for k in range(3))
                odd.append(m0 + m1)
                even.append(m1 - m2)
            for k, (m0, m1, m2) in enumerate((even, odd)):
                y[4 * b + 2 * k + 1, :, cols_t] = m0 + m1
                y[4 * b + 2 * k, :, cols_t] = m1 - m2
            return c

        lax.fori_loop(0, outs, join, 0)

    @pl.when(low < span)
    def _():
        pad = KT + JT
        x2[0:pad] = jnp.zeros((pad, SEG, cols), F32)

        def mask(j, c):
            for t in range(tiles):
                cols_t = slice(t * LANES, (t + 1) * LANES)
                v = x_ref[t, pl.ds(KTAP + j, SEG, stride=span), :]
                x2[pad + j, :, cols_t] = jnp.where(inner & (j >= begin), v, 0.0)
            return c

        lax.fori_loop(0, span, mask, 0)

        def widen2(g, c):
            w = taps_ref[pl.ds(pl.multiple_of(g * 16, 16), 16), :].astype(F32)
            for r in range(16):
                w2[16 * g + r] = jnp.broadcast_to(w[r : r + 1, :], (SEG, cols))
            return c

        lax.fori_loop(0, span // 16, widen2, 0)
        for t in range(tiles):
            cols_t = slice(t * LANES, (t + 1) * LANES)

            def outputs(jt, c, cols_t=cols_t):
                j0 = jt * JT

                def taps(g, accs):
                    k0 = g * KT
                    at = pad + j0 - k0 - (KT - 1)
                    xv = [x2[at + n, :, cols_t] for n in range(JT + KT - 1)]
                    wv = [w2[k0 + n, :, cols_t] for n in range(KT)]
                    return accumulate(accs, xv, wv)

                reach = j0 + JT - low
                accs = lax.fori_loop(
                    0,
                    (reach + KT - 1) // KT,
                    taps,
                    tuple(jnp.zeros((SEG, LANES), F32) for _ in range(JT)),
                )
                for j in range(JT):
                    here = y[j0 + j, :, cols_t]
                    y[j0 + j, :, cols_t] = jnp.where(inner & (j0 + j >= begin), accs[j], here)
                return c

            lax.fori_loop(low // JT, span // JT, outputs, 0)

    def collect(j, c):
        for t in range(tiles):
            cols_t = slice(t * LANES, (t + 1) * LANES)
            y2[t, pl.ds(j, SEG, stride=span), :] = y[j, :, cols_t]
        return c

    lax.fori_loop(0, span, collect, 0, unroll=4)

    def gating(r, c):
        at = pl.ds(pl.multiple_of(r * 64, 64), 64)
        for t in range(tiles):
            cols_t = slice(t * LANES, (t + 1) * LANES)
            g = gate_ref[at, cols_t].astype(F32)
            out_ref[at, cols_t] = (y2[t, at, :] * (g / (1.0 + jnp.exp(-g)))).astype(BF16)
        return c

    lax.fori_loop(0, rows // 64, gating, 0)


def convolution(starts, own, rim_p, rim_o, taps, gate):
    rows, cols = own.shape
    span = rows // SEG
    quarter, outs = KTAP // 4, span // 4
    tiles = cols // LANES
    return pl.pallas_call(
        functools.partial(conv_kernel, starts.shape[0]),
        out_shape=jax.ShapeDtypeStruct((rows, cols), BF16),
        in_specs=[SMEM] + [VMEM] * 5,
        out_specs=VMEM,
        scratch_shapes=[
            pltpu.VMEM((tiles, KTAP + rows, LANES), F32),
            pltpu.VMEM((9, quarter - 1 + outs, SEG, cols), F32),
            pltpu.VMEM((9, quarter, SEG, cols), F32),
            pltpu.VMEM((9, outs, SEG, LANES), F32),
            pltpu.VMEM((span, SEG, cols), F32),
            pltpu.VMEM((KT + JT + span, SEG, cols), F32),
            pltpu.VMEM((span, SEG, cols), F32),
            pltpu.VMEM((tiles, rows, LANES), F32),
        ],
        compiler_params=limit(20),
        cost_estimate=pl.CostEstimate(
            flops=40 * rows * cols * KTAP, bytes_accessed=8 * rows * cols, transcendentals=rows * cols
        ),
    )(starts, own, rim_p, rim_o, taps, gate)


def body(
    tokens,
    norm_gain,
    w_query,
    w_key,
    w_value,
    w_out,
    conv_in_w,
    conv_gate_w,
    conv_taps,
    conv_out_w,
    chain_starts,
    block_lists,
    block_counts,
):
    shards = lax.axis_size("seq")

    after = lax.optimization_barrier
    mine, yours, normed, half, w_query, w_key, w_value, conv_in_w, conv_gate_w = plan(
        block_lists, tokens, norm_gain, (w_query, w_key, w_value, conv_in_w, conv_gate_w)
    )
    to_asking = flat_pairs(shards, lambda i, h: i + (-2 if h == 0 else 2))
    to_asked = flat_pairs(shards, lambda i, h: i + (2 if h == 0 else -2))
    to_partner = flat_pairs(shards, lambda i, h: i ^ 1)
    to_other = flat_pairs(shards, lambda i, h: i + (2 if i % 2 == 0 else -2))
    chunks = [half[:BLK], half[BLK:]]
    partner, other = [None] * 2, [None] * 2
    for n in range(2):
        partner[n] = lax.ppermute(chunks[n], AXES, to_partner)
    asked = lax.ppermute(mine, AXES, to_asked)

    scale = math.log2(math.e) / math.sqrt(HD)
    queries, k_own, v_own = own_project(normed, (w_query, w_key, w_value), (scale, 1.0, 1.0))
    asked, k_own = after((asked, k_own))
    picked = pick(asked, (normed,))
    far = lax.ppermute(picked, AXES, to_asking)
    conv_input, conv_gate = own_project(normed, (conv_in_w, conv_gate_w), (1.0, 1.0))
    for n in range(2):
        other[n] = lax.ppermute(partner[n], AXES, to_other)
    partner += [swap(part) for part in partner]

    context = (chain_starts, block_lists, block_counts, mine, yours)
    *state, rim_p = attention(
        context, queries, (k_own, v_own), partner, (w_key, w_value, conv_in_w)
    )
    other, far, state = after((other, far, state))
    other += [swap(part) for part in other]
    far_s = swap(far)
    farther = lax.ppermute(pick(asked, (*partner, *other)), AXES, to_asking)

    k_o, v_o, rim_o = other_project(other, w_key, w_value, conv_in_w)
    gated = convolution(chain_starts, conv_input, rim_p, rim_o, conv_taps, conv_gate)
    farther, gated, k_o, v_o = after((farther, gated, k_o, v_o))
    theirs, ours = attention(
        context,
        queries,
        (k_o, v_o),
        (far, far_s, farther, swap(farther)),
        (w_key, w_value),
        (*state, gated, w_out, conv_out_w),
    )
    return (ours + swap(theirs).astype(F32)).astype(BF16)


def solution(mesh):
    return jax.shard_map(
        body,
        mesh=mesh,
        in_specs=(
            P("seq", None),
            P(),
            P(None, "head"),
            P(None, "head"),
            P(None, "head"),
            P("head", None),
            P(None, "head"),
            P(None, "head"),
            P(None, "head"),
            P("head", None),
            P(),
            P("seq", None),
            P("seq"),
        ),
        out_specs=P(("seq", "head"), None),
        check_vma=False,
    )
```

```python
import functools
import math

import jax
import jax.numpy as jnp
from jax import lax
from jax.experimental import pallas as pl
from jax.experimental.pallas import tpu as pltpu
from jax.sharding import PartitionSpec as P


HD = 64
KTAP = 128
BLK = 128
HALF = 512
NB = 4
LANES = 128
AXES = ("seq", "head")
NEG = -1e30
F32 = jnp.float32
BF16 = jnp.bfloat16


def flat_pairs(count, target):
    pairs = []
    for i in range(count):
        for h in range(2):
            j = target(i, h)
            if 0 <= j < count:
                pairs.append((2 * i + h, 2 * j + h))
    return pairs


def swap(value):
    return lax.ppermute(value, "head", [(0, 1), (1, 0)])


def dot(a, b):
    return jnp.dot(a, b, preferred_element_type=F32)


SMEM = pl.BlockSpec(memory_space=pltpu.SMEM)
VMEM = pl.BlockSpec(memory_space=pltpu.VMEM)
ANY = pl.BlockSpec(memory_space=pl.ANY)


def limit(mib):
    return pltpu.CompilerParams(vmem_limit_bytes=mib << 20)


def in_hbm(value):
    return pltpu.with_memory_space_constraint(value, pltpu.HBM)


PIECES = 4


def plan_kernel(per_shard, nweights, lists_in, tokens, gain_in, *refs):
    weights, refs = refs[:nweights], refs[nweights:]
    mine, yours, normed, half, *refs = refs
    kept, (lists, gain, rows, sem) = refs[:nweights], refs[nweights:]
    me, core = lax.axis_index("seq"), lax.axis_index("head")
    size = tokens.shape[0] // PIECES
    copies = [
        pltpu.make_async_copy(
            tokens.at[pl.ds(n * size, size)], rows.at[pl.ds(n * size, size)], sem.at[n]
        )
        for n in range(PIECES)
    ]
    copies.append(pltpu.make_async_copy(lists_in, lists, sem.at[PIECES]))
    copies.append(pltpu.make_async_copy(gain_in, gain, sem.at[PIECES + 1]))
    for n in range(nweights):
        copies.append(pltpu.make_async_copy(weights[n], kept[n], sem.at[PIECES + 2 + n]))
    for copy in copies:
        copy.start()
    copies[PIECES + 1].wait()
    g = jnp.broadcast_to(gain[...].reshape(1, -1), (32, normed.shape[1]))

    def norm(r, c):
        here = pl.ds(pl.multiple_of(r * 32, 32), 32)
        x = rows[here, :].astype(F32)
        x = x * lax.rsqrt(jnp.mean(x * x, axis=1, keepdims=True) + 1e-05) * g
        normed[here, :] = x.astype(BF16)
        return c

    for n in range(PIECES):
        copies[n].wait()
        lax.fori_loop(n * size // 32, (n + 1) * size // 32, norm, 0)
    copies[PIECES].wait()

    def wanted(distance):
        low = (me + distance) * per_shard
        found = jnp.int32(0)
        for q in range(per_shard):
            for m in range(NB):
                local = lists[q, m] - low
                found = jnp.where((local >= 0) & (local < per_shard), local, found)
        return found

    side = 1 - 2 * core
    for n in range(2):
        mine[n] = wanted(side * (n + 2))
        yours[n] = wanted(-side * (n + 2))
    count = half.shape[0]
    half[...] = normed[pl.ds(pl.multiple_of(core * count, count), count), :]
    for copy in copies[PIECES + 2 :]:
        copy.wait()


def plan(lists, tokens, gain, weights):
    rows, cols = tokens.shape
    pair = jax.ShapeDtypeStruct((2,), jnp.int32)
    return pl.pallas_call(
        functools.partial(plan_kernel, rows // BLK, len(weights)),
        out_shape=[
            pair,
            pair,
            jax.ShapeDtypeStruct((rows, cols), BF16),
            jax.ShapeDtypeStruct((rows // 2, cols), BF16),
        ]
        + [jax.ShapeDtypeStruct(w.shape, BF16) for w in weights],
        in_specs=[ANY] * (3 + len(weights)),
        out_specs=[SMEM, SMEM] + [VMEM] * (2 + len(weights)),
        scratch_shapes=[
            pltpu.SMEM(lists.shape, jnp.int32),
            pltpu.VMEM(gain.shape, F32),
            pltpu.VMEM((rows, cols), BF16),
            pltpu.SemaphoreType.DMA((PIECES + 2 + len(weights),)),
        ],
        compiler_params=limit(14),
        name="plan",
    )(in_hbm(lists), in_hbm(tokens), in_hbm(gain), *[in_hbm(w) for w in weights])


def pick_own_kernel(asked, own, out):
    out[...] = own[pl.ds(pl.multiple_of(asked[0] * BLK, BLK), BLK), :]


def pick_other_kernel(asked, *refs):
    *parts, out = refs
    me, core = lax.axis_index("seq"), lax.axis_index("head")
    count = len(parts) // 2
    blocks = parts[0].shape[0] // BLK
    use_partner = (me % 2) == core
    slot = (asked[1] + core * (count * blocks // 2)) % (count * blocks)
    held = slot // blocks + jnp.where(use_partner, 0, count)
    here = pl.ds(pl.multiple_of((slot % blocks) * BLK, BLK), BLK)
    for k, ref in enumerate(parts):

        @pl.when(held == k)
        def _(ref=ref):
            out[...] = ref[here, :]


def pick(asked, sources):
    if len(sources) == 1:
        kernel = pick_own_kernel
    else:
        kernel = pick_other_kernel
    return pl.pallas_call(
        kernel,
        out_shape=jax.ShapeDtypeStruct((BLK, sources[0].shape[1]), BF16),
        in_specs=[SMEM] + [VMEM] * len(sources),
        out_specs=VMEM,
        compiler_params=limit(6),
        name="pick",
    )(asked, *sources)


def rim_rows(parts):
    mine, swapped = parts[len(parts) // 2 - 1], parts[-1]
    last = slice(mine.shape[0] - KTAP, mine.shape[0])
    return jnp.where(lax.axis_index("head") == 1, mine[last, :], swapped[last, :])


def own_kernel(scale, x_ref, *refs):
    count = len(refs) // 2
    weights, outs = refs[:count], refs[count:]
    rows = x_ref.shape[0]
    for n in range(count):
        y = dot(x_ref[...], weights[n][...])
        if n == 0 and scale is not None:
            y = (y * scale).astype(BF16)
            low = lax.broadcasted_iota(jnp.int32, y.shape, 1) % LANES < HD
            outs[n][:rows, :] = jnp.where(low, y, jnp.zeros_like(y))
            outs[n][rows:, :] = jnp.where(low, jnp.zeros_like(y), y)
        else:
            outs[n][...] = y.astype(BF16)


def own_project(x, weights, scale=None):
    rows, cols = x.shape
    outs = [jax.ShapeDtypeStruct((rows, w.shape[1]), BF16) for w in weights]
    if scale is not None:
        outs[0] = jax.ShapeDtypeStruct((2 * rows, weights[0].shape[1]), BF16)
    flops = sum(2 * rows * cols * w.shape[1] for w in weights)
    return pl.pallas_call(
        functools.partial(own_kernel, scale),
        out_shape=outs,
        in_specs=[VMEM] * (1 + len(weights)),
        out_specs=[VMEM] * len(outs),
        compiler_params=limit(14),
        cost_estimate=pl.CostEstimate(
            flops=flops, bytes_accessed=sum(w.size * 2 for w in weights), transcendentals=0
        ),
        name="own_project",
    )(x, *weights)


def other_kernel(*refs):
    *parts, wk, wv, k_ref, v_ref = refs
    x = jnp.concatenate([part[...] for part in parts], axis=0)
    k_ref[...] = dot(x, wk[...]).astype(BF16)
    v_ref[...] = dot(x, wv[...]).astype(BF16)


def other_project(parts, wk, wv):
    rows, cols = sum(part.shape[0] for part in parts), parts[0].shape[1]
    return pl.pallas_call(
        other_kernel,
        out_shape=[jax.ShapeDtypeStruct((rows, w.shape[1]), BF16) for w in (wk, wv)],
        in_specs=[VMEM] * (2 + len(parts)),
        out_specs=[VMEM] * 2,
        compiler_params=limit(10),
        cost_estimate=pl.CostEstimate(
            flops=4 * rows * cols * wk.shape[1], bytes_accessed=4 * wk.size, transcendentals=0
        ),
        name="other_project",
    )(*parts, wk, wv)


BIG = 1 << 30
FAR = 1 << 20


def attention_kernel(
    first,
    fresh_parts,
    nch,
    per_shard,
    kblocks,
    starts,
    lists,
    counts,
    mine,
    yours,
    q_ref,
    *refs,
):
    k_in, v_in, *refs = refs
    new, (wk, wv, *refs) = refs[:fresh_parts], refs[fresh_parts:]
    if first:
        wc_in, o_ref, l_ref, mx_ref, rim_ref, *refs = refs
    else:
        o_ref, l_ref, mx_ref, g_ref, wo, wco, theirs, ours, *refs = refs
    k_all, v_all, s_buf, m_buf, bias, k_chain, i_chain, gblk, flag, ids, around, *refs = refs
    a_ref = None if first else refs[0]
    pairs = q_ref.shape[1] // LANES
    held = k_in.shape[0]
    k_all[:held] = k_in[...]
    v_all[:held] = v_in[...]
    fresh = jnp.concatenate([part[...] for part in new], axis=0)
    k_all[held:] = dot(fresh, wk[...]).astype(BF16)
    v_all[held:] = dot(fresh, wv[...]).astype(BF16)
    if first:
        rim_ref[...] = dot(rim_rows(new), wc_in[...]).astype(BF16)

    me, core = lax.axis_index("seq"), lax.axis_index("head")
    shards = lax.axis_size("seq")
    step = 1 - 2 * (me % 2)
    side = 1 - 2 * core
    turn = core * (per_shard // 2)
    own = me * per_shard

    def block_of(shard, local):
        return jnp.where((shard >= 0) & (shard < shards), shard * per_shard + local, -FAR)

    for p in range(per_shard):
        local = (turn + p) % per_shard
        if first:
            gblk[p] = own + p
            gblk[per_shard + p] = block_of(me + step, local)
        else:
            gblk[p] = block_of(me - step, local)
    if not first:
        for n in range(2):
            gblk[per_shard + 2 * n] = block_of(me + side * (n + 2), mine[n])
            gblk[per_shard + 2 * n + 1] = block_of(me - side * (n + 2), yours[n])

    def slot_of(block):
        shard = block // per_shard
        away = shard - me
        near_slot = (block % per_shard - turn) % per_shard
        if first:
            return jnp.where(away == step, per_shard + near_slot, kblocks)
        far_slot = per_shard + 2 * (jnp.abs(away) - 2) + jnp.where(away * side > 0, 0, 1)
        return jnp.where(
            away == -step, near_slot, jnp.where(jnp.abs(away) >= 2, far_slot, kblocks)
        )

    def chain_of(pos):
        return lax.fori_loop(
            0,
            nch,
            lambda c, n: n + jnp.where(starts[c] <= pos, 1, 0),
            jnp.full(pos.shape, -1, jnp.int32),
        )

    lane = lax.broadcasted_iota(jnp.int32, (BLK, LANES), 1)
    row = lax.broadcasted_iota(jnp.int32, (BLK, LANES), 0)
    low = lane < HD
    for b in range(kblocks):
        k_chain[pl.ds(b, 1), :] = gblk[b] * BLK + lane[0:1, :]
    k_chain[...] = chain_of(k_chain[...])
    bias[kblocks] = jnp.full((BLK, LANES), NEG, F32)

    def scan(c, found):
        s, out = starts[c], []
        for n in range(per_shard):
            q_first = (own + n) * BLK
            chain, begin, end, after = found[4 * n : 4 * n + 4]
            ahead = s <= q_first
            out += [
                chain + ahead.astype(jnp.int32),
                jnp.where(ahead, jnp.maximum(begin, s), begin),
                jnp.where(ahead, end, jnp.minimum(end, s)),
                jnp.where(s > q_first + BLK - 1, jnp.minimum(after, s), after),
            ]
        return tuple(out)

    none = (jnp.int32(-1), jnp.int32(0), jnp.int32(BIG), jnp.int32(BIG))
    for n, value in enumerate(lax.fori_loop(0, nch, scan, none * per_shard)):
        around[n] = value

    def one_block(qb, carry):
        gq = own + qb
        q_first = gq * BLK
        q_last = q_first + BLK - 1
        chain, begin, end, after = (around[4 * qb + n] for n in range(4))
        i_chain[...] = jnp.where(q_first + row >= end, chain + 1, chain)
        q_rows = pl.ds(pl.multiple_of(qb * BLK, BLK), BLK)
        q_rows_high = pl.ds(pl.multiple_of((per_shard + qb) * BLK, BLK), BLK)

        for b in range(kblocks + 1):
            flag[b] = 0

        def mark(m, c):
            flag[slot_of(lists[qb, m])] = 1
            return c

        lax.fori_loop(0, counts[qb], mark, 0)

        count = jnp.int32(0)
        for b in range(kblocks):
            gk = gblk[b]
            k_first = gk * BLK
            k_last = k_first + BLK - 1
            away = gk - gq
            near = (jnp.abs(away) * BLK <= HALF) & (k_last >= begin) & (k_first < after)
            listed = flag[b]
            one_chain = (k_first >= begin) & (jnp.maximum(k_last, q_last) < end)
            active = near | ((listed == 1) & jnp.logical_not(one_chain))
            ids[count] = b
            count = count + active.astype(jnp.int32)
            same = i_chain[...] == k_chain[b : b + 1, :]
            if first and b < per_shard:
                bias[b] = jnp.where(same, 0.0, NEG)
                continue
            relative = away * BLK + lane - row
            in_window = jnp.where((relative >= -HALF) & (relative < HALF), 0.0, NEG)
            in_list = jnp.where(listed == 1, 0.0, NEG)
            bias[b] = jnp.where(same, in_window, in_list)
        ids[count] = kblocks
        ids[count + 1] = kblocks
        steps = jnp.maximum((count + 1) // 2, 1)

        def attend(steps):
            masks = [bias[ids[n]] for n in range(2 * steps)]
            rows_of = [
                pl.ds(pl.multiple_of(jnp.minimum(ids[n], kblocks - 1) * BLK, BLK), BLK)
                for n in range(2 * steps)
            ]

            def scores(p):
                cols = slice(p * LANES, (p + 1) * LANES)
                if first:
                    m = None
                else:
                    old = mx_ref[q_rows, cols]
                    turned = pltpu.roll(old, HD, 1)
                    m = jnp.concatenate([jnp.where(low, old, turned), jnp.where(low, turned, old)], 0)
                q = jnp.concatenate([q_ref[q_rows, cols], q_ref[q_rows_high, cols]], axis=0)
                for n in range(steps):
                    k = jnp.concatenate(
                        [k_all[rows_of[2 * n], cols], k_all[rows_of[2 * n + 1], cols]], axis=0
                    )
                    s = lax.dot_general(
                        q, k, (((1,), (1,)), ((), ())), preferred_element_type=F32
                    )
                    mask = jnp.concatenate([masks[2 * n], masks[2 * n + 1]], axis=1)
                    s = s + jnp.concatenate([mask, mask], axis=0)
                    s_buf[p, n] = s
                    top = jnp.maximum(s[:, :LANES], s[:, LANES:])
                    m = top if m is None else jnp.maximum(m, top)
                m_buf[p] = jnp.broadcast_to(jnp.max(m, axis=1, keepdims=True), (2 * BLK, LANES))

            def sums(p):
                cols = slice(p * LANES, (p + 1) * LANES)
                m = m_buf[p]
                m2 = jnp.concatenate([m, m], axis=1)
                e = jnp.concatenate(
                    [jnp.exp2(s_buf[p, n] - m2).astype(BF16) for n in range(steps)], axis=1
                )
                v = jnp.concatenate([v_all[here, cols] for here in rows_of], axis=0)
                v = jnp.concatenate([v, jnp.ones_like(v)], axis=1)
                y = dot(e, v)
                o = jnp.where(low, y[:BLK, :LANES], y[BLK:, :LANES])
                l = jnp.where(low, y[:BLK, LANES:], y[BLK:, LANES:])
                m = jnp.where(low, m[:BLK], m[BLK:])
                if first:
                    o_ref[q_rows, cols] = o
                    l_ref[q_rows, cols] = l
                    mx_ref[q_rows, cols] = m
                else:
                    scale = jnp.exp2(mx_ref[q_rows, cols] - m)
                    o = o + o_ref[q_rows, cols] * scale
                    l = l + l_ref[q_rows, cols] * scale
                    a_ref[q_rows, cols] = (o / l).astype(BF16)

            scores(0)
            for p in range(pairs):
                if p + 1 < pairs:
                    scores(p + 1)
                sums(p)

        for n in range(1, kblocks // 2 + 1):

            @pl.when(steps == n)
            def _(n=n):
                attend(n)

        return carry

    lax.fori_loop(0, per_shard, one_block, 0)
    if not first:
        rows = ours.shape[0]
        for half, out in ((1 - core, theirs), (core, ours)):
            here = pl.ds(pl.multiple_of(half * rows, rows), rows)
            y = dot(a_ref[here, :], wo[...]) + dot(g_ref[here, :], wco[...])
            out[...] = y.astype(out.dtype)


def attention(context, queries, kv, new, weights, finish=None):
    rows, cols = kv[0].shape
    pairs = cols // LANES
    fresh = sum(part.shape[0] for part in new)
    keys = kv[0].shape[0] + fresh
    kblocks = keys // BLK
    steps = (kblocks + 1) // 2
    first = finish is None
    sums = jax.ShapeDtypeStruct((rows, cols), F32)
    if first:
        extra, more = (), []
        out_shape = [sums] * 3 + [jax.ShapeDtypeStruct((KTAP, weights[2].shape[1]), BF16)]
    else:
        extra, more = finish, [pltpu.VMEM((rows, cols), BF16)]
        wide = finish[4].shape[1]
        out_shape = [jax.ShapeDtypeStruct((rows // 2, wide), t) for t in (BF16, F32)]
    operands = (queries, *kv, *new, *weights, *extra)
    return pl.pallas_call(
        functools.partial(
            attention_kernel, first, len(new), context[0].shape[0], rows // BLK, kblocks
        ),
        out_shape=out_shape,
        in_specs=[SMEM] * len(context) + [VMEM] * len(operands),
        out_specs=[VMEM] * len(out_shape),
        scratch_shapes=[pltpu.VMEM((keys, cols), BF16)] * 2
        + [
            pltpu.VMEM((pairs, steps, 2 * BLK, 2 * BLK), F32),
            pltpu.VMEM((pairs, 2 * BLK, LANES), F32),
            pltpu.VMEM((kblocks + 1, BLK, LANES), F32),
            pltpu.VMEM((kblocks, LANES), jnp.int32),
            pltpu.VMEM((BLK, LANES), jnp.int32),
            pltpu.SMEM((kblocks,), jnp.int32),
            pltpu.SMEM((kblocks + 1,), jnp.int32),
            pltpu.SMEM((kblocks + 2,), jnp.int32),
            pltpu.SMEM((4 * rows // BLK,), jnp.int32),
        ]
        + more,
        compiler_params=limit(32),
        cost_estimate=pl.CostEstimate(
            flops=4 * rows * keys * cols, bytes_accessed=4 * keys * cols, transcendentals=rows * keys
        ),
        name="attention",
    )(*context, *operands)


SEG = 8
KT = 8


def accumulate(accs, xv, wv):
    accs, taps = list(accs), len(wv)
    for n in range(taps):
        for j in range(len(accs)):
            accs[j] = accs[j] + xv[j - n + taps - 1] * wv[n]
    return tuple(accs)


def conv_kernel(
    nch, starts, own_ref, rim_p, last, last_s, wc, taps_ref, gate_ref, out_ref, x_ref, xs, ws, ms, y, xl, tf, y2
):
    rows, cols = own_ref.shape
    span = rows // SEG
    tiles = cols // LANES
    quarter, outs = KTAP // 4, span // 4
    me = lax.axis_index("seq")
    first = me * rows

    seg = lax.broadcasted_iota(jnp.int32, (SEG, LANES), 0)
    seg_first = first + seg * span

    def latest(c, begin):
        s = starts[c]
        return jnp.where(s < seg_first + span, jnp.maximum(begin, s), begin)

    begin = lax.fori_loop(0, nch, latest, jnp.zeros((SEG, LANES), jnp.int32))
    begin = begin - seg_first
    inner = begin > 0
    outer_begin = jnp.where(inner, -(1 << 30), begin)

    rim_o = dot(rim_rows((last, last_s)), wc[...]).astype(BF16)
    for t in range(tiles):
        cols_t = slice(t * LANES, (t + 1) * LANES)
        x_ref[t, 0:KTAP, :] = jnp.where(me % 2 == 1, rim_p[:, cols_t], rim_o[:, cols_t]).astype(F32)
        x_ref[t, pl.ds(KTAP, rows), :] = own_ref[:, cols_t].astype(F32)
        x_ref[t, pl.ds(KTAP + rows, 8), :] = jnp.zeros((8, LANES), F32)

    def row_of(j, t):
        v = x_ref[t, pl.ds(KTAP + j, SEG, stride=span), :]
        return jnp.where(j >= outer_begin, v, 0.0)

    def spread(n, before):
        j = 4 * (n - (quarter - 1))
        after = []
        for t in range(tiles):
            cols_t = slice(t * LANES, (t + 1) * LANES)
            a3, a2, a1 = before[3 * t : 3 * t + 3]
            b0, b1, b2, b3 = (row_of(j + k, t) for k in range(4))
            for s, (early, here, late) in enumerate(
                ((a1 - a2, b1 - b0, b3 - b2), (a2, b0, b2), (a2 - a3, b0 - a1, b2 - b1))
            ):
                xs[3 * s, n, :, cols_t] = late - here
                xs[3 * s + 1, n, :, cols_t] = here
                xs[3 * s + 2, n, :, cols_t] = here - early
            after += [b1, b2, b3]
        return tuple(after)

    start = 4 * (1 - quarter)
    lax.fori_loop(
        0,
        quarter + outs,
        spread,
        tuple(row_of(start + k, t) for t in range(tiles) for k in (-3, -2, -1)),
        unroll=2,
    )

    def widen(g, c):
        here = pl.ds(pl.multiple_of(g * 16, 16), 16)
        w = taps_ref[here, :].astype(F32)
        for t in range(tiles):
            tf[t, here, :] = w[:, t * LANES : (t + 1) * LANES]
        for r in range(4):
            w0, w1, w2, w3 = (w[4 * r + k : 4 * r + k + 1, :] for k in range(4))
            for s, (u, v) in enumerate(((w0, w2), (w0 + w1, w2 + w3), (w1, w3))):
                for k, value in enumerate((u, u + v, v)):
                    ws[3 * s + k, 4 * g + r] = jnp.broadcast_to(value, (SEG, cols))
        return c

    lax.fori_loop(0, KTAP // 16, widen, 0)

    for t in range(tiles):
        cols_t = slice(t * LANES, (t + 1) * LANES)

        def filtered(f, c, cols_t=cols_t):
            accs = tuple(jnp.zeros((SEG, LANES), F32) for _ in range(outs))
            for k0 in range(0, quarter, KT):
                at = quarter - k0 - KT
                xv = [xs[f, at + n, :, cols_t] for n in range(outs + KT - 1)]
                wv = [ws[f, k0 + n, :, cols_t] for n in range(KT)]
                accs = accumulate(accs, xv, wv)
            for j in range(outs):
                ms[f, j] = accs[j]
            return c

        lax.fori_loop(0, 9, filtered, 0)

        def join(b, c, cols_t=cols_t):
            odd, even = [], []
            for s in range(3):
                m0, m1, m2 = (ms[3 * s + k, b] for k in range(3))
                odd.append(m0 + m1)
                even.append(m1 - m2)
            for k, (m0, m1, m2) in enumerate((even, odd)):
                y[4 * b + 2 * k + 1, :, cols_t] = m0 + m1
                y[4 * b + 2 * k, :, cols_t] = m1 - m2
            return c

        lax.fori_loop(0, outs, join, 0)

    def collect(j, c):
        for t in range(tiles):
            cols_t = slice(t * LANES, (t + 1) * LANES)
            y2[t, pl.ds(j, SEG, stride=span), :] = y[j, :, cols_t]
        return c

    lax.fori_loop(0, span, collect, 0, unroll=4)

    eighth = span // SEG
    xl[:, 0:span, :] = jnp.zeros((tiles, span, LANES), F32)
    row_in = lax.broadcasted_iota(jnp.int32, (span, LANES), 0)

    def repair(c, carry):
        at = starts[c] - first
        seg_at, from_row = at // span, lax.rem(at, span)

        @pl.when((at > 0) & (at < rows) & (from_row > 0))
        def _():
            base = pl.multiple_of(seg_at * span, span)
            for t in range(tiles):
                x = x_ref[t, pl.ds(KTAP + base, span), :]
                xl[t, span:, :] = jnp.where(row_in >= from_row, x, 0.0)
            for t in range(tiles):

                def taps(g, accs, t=t):
                    k0 = pl.multiple_of(g * KT, KT)
                    lo = span - k0 - (KT - 1)
                    xv = [
                        xl[t, pl.ds(lo + n, SEG, stride=eighth), :] for n in range(eighth + KT - 1)
                    ]
                    w = tf[t, pl.ds(k0, KT), :]
                    wv = [jnp.broadcast_to(w[n : n + 1, :], (SEG, LANES)) for n in range(KT)]
                    return accumulate(accs, xv, wv)

                accs = lax.fori_loop(
                    0,
                    (span - from_row + KT - 1) // KT,
                    taps,
                    tuple(jnp.zeros((SEG, LANES), F32) for _ in range(eighth)),
                )
                part = lax.broadcasted_iota(jnp.int32, (SEG, LANES), 0) * eighth
                for j in range(eighth):
                    here = pl.ds(base + j, SEG, stride=eighth)
                    y2[t, here, :] = jnp.where(part + j >= from_row, accs[j], y2[t, here, :])

        return carry

    lax.fori_loop(0, nch, repair, 0)

    def gating(r, c):
        at = pl.ds(pl.multiple_of(r * 64, 64), 64)
        for t in range(tiles):
            cols_t = slice(t * LANES, (t + 1) * LANES)
            g = gate_ref[at, cols_t].astype(F32)
            out_ref[at, cols_t] = (y2[t, at, :] * (g / (1.0 + jnp.exp(-g)))).astype(BF16)
        return c

    lax.fori_loop(0, rows // 64, gating, 0)


def convolution(starts, own, rim_p, last, last_s, wc, taps, gate):
    rows, cols = own.shape
    span = rows // SEG
    quarter, outs = KTAP // 4, span // 4
    tiles = cols // LANES
    return pl.pallas_call(
        functools.partial(conv_kernel, starts.shape[0]),
        out_shape=jax.ShapeDtypeStruct((rows, cols), BF16),
        in_specs=[SMEM] + [VMEM] * 7,
        out_specs=VMEM,
        scratch_shapes=[
            pltpu.VMEM((tiles, KTAP + rows + 8, LANES), F32),
            pltpu.VMEM((9, quarter + outs, SEG, cols), F32),
            pltpu.VMEM((9, quarter, SEG, cols), F32),
            pltpu.VMEM((9, outs, SEG, LANES), F32),
            pltpu.VMEM((span, SEG, cols), F32),
            pltpu.VMEM((tiles, 2 * span, LANES), F32),
            pltpu.VMEM((tiles, KTAP, LANES), F32),
            pltpu.VMEM((tiles, rows, LANES), F32),
        ],
        compiler_params=limit(20),
        cost_estimate=pl.CostEstimate(
            flops=40 * rows * cols * KTAP, bytes_accessed=8 * rows * cols, transcendentals=rows * cols
        ),
    )(starts, own, rim_p, last, last_s, wc, taps, gate)


def body(
    tokens,
    norm_gain,
    w_query,
    w_key,
    w_value,
    w_out,
    conv_in_w,
    conv_gate_w,
    conv_taps,
    conv_out_w,
    chain_starts,
    block_lists,
    block_counts,
):
    shards = lax.axis_size("seq")

    after = lax.optimization_barrier
    mine, yours, normed, half, w_query, w_key, w_value, conv_in_w, conv_gate_w = plan(
        block_lists, tokens, norm_gain, (w_query, w_key, w_value, conv_in_w, conv_gate_w)
    )
    to_asking = flat_pairs(shards, lambda i, h: i + (-2 if h == 0 else 2))
    to_asked = flat_pairs(shards, lambda i, h: i + (2 if h == 0 else -2))
    to_partner = flat_pairs(shards, lambda i, h: i ^ 1)
    to_other = flat_pairs(shards, lambda i, h: i + (2 if i % 2 == 0 else -2))
    chunks = [half[:BLK], half[BLK:]]
    partner, other = [None] * 2, [None] * 2
    for n in range(2):
        partner[n] = lax.ppermute(chunks[n], AXES, to_partner)
    asked = lax.ppermute(mine, AXES, to_asked)

    scale = math.log2(math.e) / math.sqrt(HD)
    queries, k_own, v_own = own_project(normed, (w_query, w_key, w_value), scale)
    asked, k_own = after((asked, k_own))
    picked = pick(asked, (normed,))
    far = lax.ppermute(picked, AXES, to_asking)
    conv_input, conv_gate = own_project(normed, (conv_in_w, conv_gate_w))
    for n in range(2):
        other[n] = lax.ppermute(partner[n], AXES, to_other)
    partner += [swap(part) for part in partner]

    context = (chain_starts, block_lists, block_counts, mine, yours)
    *state, rim_p = attention(
        context, queries, (k_own, v_own), partner, (w_key, w_value, conv_in_w)
    )
    other, far, state = after((other, far, state))
    other += [swap(part) for part in other]
    far_s = swap(far)
    farther = lax.ppermute(pick(asked, (*partner, *other)), AXES, to_asking)

    gated = convolution(
        chain_starts, conv_input, rim_p, other[1], other[3], conv_in_w, conv_taps, conv_gate
    )
    farther, gated, other = after((farther, gated, other))
    farther_s = swap(farther)
    k_o, v_o = other_project(other, w_key, w_value)
    theirs, ours = attention(
        context,
        queries,
        (k_o, v_o),
        (far, far_s, farther, farther_s),
        (w_key, w_value),
        (*state, gated, w_out, conv_out_w),
    )
    return (ours + swap(theirs).astype(F32)).astype(BF16)


def solution(mesh):
    return jax.shard_map(
        body,
        mesh=mesh,
        in_specs=(
            P("seq", None),
            P(),
            P(None, "head"),
            P(None, "head"),
            P(None, "head"),
            P("head", None),
            P(None, "head"),
            P(None, "head"),
            P(None, "head"),
            P("head", None),
            P(),
            P("seq", None),
            P("seq"),
        ),
        out_specs=P(("seq", "head"), None),
        check_vma=False,
    )
```

```python
import functools
import math

import jax
import jax.numpy as jnp
from jax import lax
from jax.experimental import pallas as pl
from jax.experimental.pallas import tpu as pltpu
from jax.sharding import PartitionSpec as P


HD = 64
KTAP = 128
BLK = 128
HALF = 512
NB = 4
LANES = 128
AXES = ("seq", "head")
NEG = -1e30
F32 = jnp.float32
BF16 = jnp.bfloat16


def flat_pairs(count, target):
    pairs = []
    for i in range(count):
        for h in range(2):
            j = target(i, h)
            if 0 <= j < count:
                pairs.append((2 * i + h, 2 * j + h))
    return pairs


def swap(value):
    return lax.ppermute(value, "head", [(0, 1), (1, 0)])


def dot(a, b):
    return jnp.dot(a, b, preferred_element_type=F32)


SMEM = pl.BlockSpec(memory_space=pltpu.SMEM)
VMEM = pl.BlockSpec(memory_space=pltpu.VMEM)
ANY = pl.BlockSpec(memory_space=pl.ANY)


def limit(mib):
    return pltpu.CompilerParams(vmem_limit_bytes=mib << 20)


def in_hbm(value):
    return pltpu.with_memory_space_constraint(value, pltpu.HBM)


PIECES = 4


def plan_kernel(per_shard, nweights, lists_in, tokens, gain_in, *refs):
    weights, refs = refs[:nweights], refs[nweights:]
    mine, yours, normed, half, *refs = refs
    every, lists, gain, rows, sem = refs
    kept, column = [], 0
    for w in weights:
        kept.append(every.at[:, pl.ds(column, w.shape[1])])
        column += w.shape[1]
    me, core = lax.axis_index("seq"), lax.axis_index("head")
    size = tokens.shape[0] // PIECES
    small = [
        pltpu.make_async_copy(lists_in, lists, sem.at[PIECES]),
        pltpu.make_async_copy(gain_in, gain, sem.at[PIECES + 1]),
    ]
    copies = [
        pltpu.make_async_copy(
            tokens.at[pl.ds(n * size, size)], rows.at[pl.ds(n * size, size)], sem.at[n]
        )
        for n in range(PIECES)
    ]
    copies += [
        pltpu.make_async_copy(weights[n], kept[n], sem.at[PIECES + 2 + n]) for n in range(nweights)
    ]
    for copy in small + copies:
        copy.start()
    for copy in small:
        copy.wait()
    g = jnp.broadcast_to(gain[...].reshape(1, -1), (32, normed.shape[1]))

    def norm(r, c):
        here = pl.ds(pl.multiple_of(r * 32, 32), 32)
        x = rows[here, :].astype(F32)
        x = x * lax.rsqrt(jnp.mean(x * x, axis=1, keepdims=True) + 1e-05) * g
        normed[here, :] = x.astype(BF16)
        return c

    for n in range(PIECES):
        copies[n].wait()
        lax.fori_loop(n * size // 32, (n + 1) * size // 32, norm, 0)

    def wanted(distance):
        low = (me + distance) * per_shard
        found = jnp.int32(0)
        for q in range(per_shard):
            for m in range(NB):
                local = lists[q, m] - low
                found = jnp.where((local >= 0) & (local < per_shard), local, found)
        return found

    side = 1 - 2 * core
    for n in range(2):
        mine[n] = wanted(side * (n + 2))
        yours[n] = wanted(-side * (n + 2))
    count = half.shape[0]
    half[...] = normed[pl.ds(pl.multiple_of(core * count, count), count), :]
    for copy in copies[PIECES:]:
        copy.wait()


def plan(lists, tokens, gain, weights):
    rows, cols = tokens.shape
    pair = jax.ShapeDtypeStruct((2,), jnp.int32)
    return pl.pallas_call(
        functools.partial(plan_kernel, rows // BLK, len(weights)),
        out_shape=[
            pair,
            pair,
            jax.ShapeDtypeStruct((rows, cols), BF16),
            jax.ShapeDtypeStruct((rows // 2, cols), BF16),
        ]
        + [jax.ShapeDtypeStruct((cols, sum(w.shape[1] for w in weights)), BF16)],
        in_specs=[ANY] * (3 + len(weights)),
        out_specs=[SMEM, SMEM] + [VMEM] * 3,
        scratch_shapes=[
            pltpu.SMEM(lists.shape, jnp.int32),
            pltpu.VMEM(gain.shape, F32),
            pltpu.VMEM((rows, cols), BF16),
            pltpu.SemaphoreType.DMA((PIECES + 2 + len(weights),)),
        ],
        compiler_params=limit(14),
        name="plan",
    )(in_hbm(lists), in_hbm(tokens), in_hbm(gain), *[in_hbm(w) for w in weights])


def pick_own_kernel(asked, own, out):
    out[...] = own[pl.ds(pl.multiple_of(asked[0] * BLK, BLK), BLK), :]


def pick_other_kernel(asked, *refs):
    *parts, out = refs
    me, core = lax.axis_index("seq"), lax.axis_index("head")
    count = len(parts) // 2
    blocks = parts[0].shape[0] // BLK
    use_partner = (me % 2) == core
    slot = (asked[1] + core * (count * blocks // 2)) % (count * blocks)
    held = slot // blocks + jnp.where(use_partner, 0, count)
    here = pl.ds(pl.multiple_of((slot % blocks) * BLK, BLK), BLK)
    for k, ref in enumerate(parts):

        @pl.when(held == k)
        def _(ref=ref):
            out[...] = ref[here, :]


def pick(asked, sources):
    if len(sources) == 1:
        kernel = pick_own_kernel
    else:
        kernel = pick_other_kernel
    return pl.pallas_call(
        kernel,
        out_shape=jax.ShapeDtypeStruct((BLK, sources[0].shape[1]), BF16),
        in_specs=[SMEM] + [VMEM] * len(sources),
        out_specs=VMEM,
        compiler_params=limit(6),
        name="pick",
    )(asked, *sources)


def rim_rows(parts):
    mine, swapped = parts[len(parts) // 2 - 1], parts[-1]
    last = slice(mine.shape[0] - KTAP, mine.shape[0])
    return jnp.where(lax.axis_index("head") == 1, mine[last, :], swapped[last, :])


WIDE = 2 * LANES


def products(x, weights, columns, outs):
    where = []
    for width, store in outs:
        where += [(store, c) for c in range(0, width, LANES)]
    total = len(where) * LANES
    for n in range(0, total, WIDE):
        last = min(n + WIDE, total)
        y = dot(x, weights[:, columns + n : columns + last])
        for c in range(n, last, LANES):
            store, column = where[c // LANES]
            store(slice(column, column + LANES), y[:, c - n : c - n + LANES])


def stored_in(ref, rows=slice(None)):
    def store(cols, y):
        ref[rows, cols] = y.astype(BF16)

    return ref.shape[1], store


def own_kernel(columns, scale, x_ref, weights, *outs):
    targets = [stored_in(out) for out in outs]
    if scale is not None:
        q_ref, rows = outs[0], x_ref.shape[0]
        low = lax.broadcasted_iota(jnp.int32, (rows, LANES), 1) < HD

        def store(cols, y):
            y = (y * scale).astype(BF16)
            q_ref[:rows, cols] = jnp.where(low, y, jnp.zeros_like(y))
            q_ref[rows:, cols] = jnp.where(low, jnp.zeros_like(y), y)

        targets[0] = (q_ref.shape[1], store)
    products(x_ref[...], weights, columns, targets)


def own_project(x, weights, columns, widths, scale=None):
    rows, cols = x.shape
    outs = [jax.ShapeDtypeStruct((rows, width), BF16) for width in widths]
    if scale is not None:
        outs[0] = jax.ShapeDtypeStruct((2 * rows, widths[0]), BF16)
    return pl.pallas_call(
        functools.partial(own_kernel, columns, scale),
        out_shape=outs,
        in_specs=[VMEM] * 2,
        out_specs=[VMEM] * len(outs),
        compiler_params=limit(16),
        cost_estimate=pl.CostEstimate(
            flops=2 * rows * cols * sum(widths), bytes_accessed=2 * cols * sum(widths), transcendentals=0
        ),
        name="own_project",
    )(x, weights)


def other_kernel(columns, *refs):
    *parts, weights, k_ref, v_ref = refs
    x = jnp.concatenate([part[...] for part in parts], axis=0)
    products(x, weights, columns, [stored_in(k_ref), stored_in(v_ref)])


def other_project(parts, weights, columns, width):
    rows, cols = sum(part.shape[0] for part in parts), parts[0].shape[1]
    return pl.pallas_call(
        functools.partial(other_kernel, columns),
        out_shape=[jax.ShapeDtypeStruct((rows, width), BF16)] * 2,
        in_specs=[VMEM] * (1 + len(parts)),
        out_specs=[VMEM] * 2,
        compiler_params=limit(14),
        cost_estimate=pl.CostEstimate(
            flops=4 * rows * cols * width, bytes_accessed=4 * cols * width, transcendentals=0
        ),
        name="other_project",
    )(*parts, weights)


BIG = 1 << 30
FAR = 1 << 20


def attention_kernel(
    stage,
    columns,
    fresh_parts,
    nch,
    per_shard,
    kblocks,
    starts,
    lists,
    counts,
    mine,
    yours,
    q_ref,
    k_in,
    v_in,
    *refs,
):
    first = stage == 0
    new, refs = refs[:fresh_parts], refs[fresh_parts:]
    if stage < 2:
        weights, *refs = refs
    if first:
        o_ref, l_ref, mx_ref, rim_ref, k_all, v_all, *refs = refs
    else:
        o_ref, l_ref, mx_ref, g_ref, wo, wco, out_ref, *refs = refs
        k_all, v_all, refs = (refs[0], refs[1], refs[2:]) if stage == 1 else (k_in, v_in, refs)
    s_buf, m_buf, bias, k_chain, i_chain, gblk, flag, ids, around, *refs = refs
    a_ref = None if first else refs[0]
    pairs = q_ref.shape[1] // LANES
    if stage < 2:
        held = k_in.shape[0]
        k_all[:held] = k_in[...]
        v_all[:held] = v_in[...]
        fresh = jnp.concatenate([part[...] for part in new], axis=0)
        rest = slice(held, None)
        products(fresh, weights, columns, [stored_in(k_all, rest), stored_in(v_all, rest)])
    if first:
        conv_columns = columns + 2 * k_in.shape[1]
        products(rim_rows(new), weights, conv_columns, [stored_in(rim_ref)])

    me, core = lax.axis_index("seq"), lax.axis_index("head")
    shards = lax.axis_size("seq")
    step = 1 - 2 * (me % 2)
    side = 1 - 2 * core
    turn = core * (per_shard // 2)
    own = me * per_shard

    def block_of(shard, local):
        return jnp.where((shard >= 0) & (shard < shards), shard * per_shard + local, -FAR)

    for p in range(per_shard):
        local = (turn + p) % per_shard
        if first:
            gblk[p] = own + p
            gblk[per_shard + p] = block_of(me + step, local)
        else:
            gblk[p] = block_of(me - step, local)
    if not first:
        for n in range(2):
            gblk[per_shard + 2 * n] = block_of(me + side * (n + 2), mine[n])
            gblk[per_shard + 2 * n + 1] = block_of(me - side * (n + 2), yours[n])

    def slot_of(block):
        shard = block // per_shard
        away = shard - me
        near_slot = (block % per_shard - turn) % per_shard
        if first:
            return jnp.where(away == step, per_shard + near_slot, kblocks)
        far_slot = per_shard + 2 * (jnp.abs(away) - 2) + jnp.where(away * side > 0, 0, 1)
        return jnp.where(
            away == -step, near_slot, jnp.where(jnp.abs(away) >= 2, far_slot, kblocks)
        )

    def chain_of(pos):
        return lax.fori_loop(
            0,
            nch,
            lambda c, n: n + jnp.where(starts[c] <= pos, 1, 0),
            jnp.full(pos.shape, -1, jnp.int32),
        )

    lane = lax.broadcasted_iota(jnp.int32, (BLK, LANES), 1)
    row = lax.broadcasted_iota(jnp.int32, (BLK, LANES), 0)
    low = lane < HD
    for b in range(kblocks):
        k_chain[pl.ds(b, 1), :] = gblk[b] * BLK + lane[0:1, :]
    k_chain[...] = chain_of(k_chain[...])
    bias[kblocks] = jnp.full((BLK, LANES), NEG, F32)

    def scan(c, found):
        s, out = starts[c], []
        for n in range(per_shard):
            q_first = (own + n) * BLK
            chain, begin, end, after = found[4 * n : 4 * n + 4]
            ahead = s <= q_first
            out += [
                chain + ahead.astype(jnp.int32),
                jnp.where(ahead, jnp.maximum(begin, s), begin),
                jnp.where(ahead, end, jnp.minimum(end, s)),
                jnp.where(s > q_first + BLK - 1, jnp.minimum(after, s), after),
            ]
        return tuple(out)

    none = (jnp.int32(-1), jnp.int32(0), jnp.int32(BIG), jnp.int32(BIG))
    for n, value in enumerate(lax.fori_loop(0, nch, scan, none * per_shard)):
        around[n] = value

    blocks = per_shard if first else per_shard // 2
    q_base = (0, (1 - core) * blocks, core * blocks)[stage]

    def one_block(t, carry):
        qb = q_base + t
        gq = own + qb
        q_first = gq * BLK
        q_last = q_first + BLK - 1
        chain, begin, end, after = (around[4 * qb + n] for n in range(4))
        i_chain[...] = jnp.where(q_first + row >= end, chain + 1, chain)
        q_rows = pl.ds(pl.multiple_of(qb * BLK, BLK), BLK)
        q_rows_high = pl.ds(pl.multiple_of((per_shard + qb) * BLK, BLK), BLK)

        for b in range(kblocks + 1):
            flag[b] = 0

        def mark(m, c):
            flag[slot_of(lists[qb, m])] = 1
            return c

        lax.fori_loop(0, counts[qb], mark, 0)

        count = jnp.int32(0)
        for b in range(kblocks):
            gk = gblk[b]
            k_first = gk * BLK
            k_last = k_first + BLK - 1
            away = gk - gq
            near = (jnp.abs(away) * BLK <= HALF) & (k_last >= begin) & (k_first < after)
            listed = flag[b]
            one_chain = (k_first >= begin) & (jnp.maximum(k_last, q_last) < end)
            active = near | ((listed == 1) & jnp.logical_not(one_chain))
            ids[count] = b
            count = count + active.astype(jnp.int32)
            same = i_chain[...] == k_chain[b : b + 1, :]
            if first and b < per_shard:
                bias[b] = jnp.where(same, 0.0, NEG)
                continue
            relative = away * BLK + lane - row
            in_window = jnp.where((relative >= -HALF) & (relative < HALF), 0.0, NEG)
            in_list = jnp.where(listed == 1, 0.0, NEG)
            bias[b] = jnp.where(same, in_window, in_list)
        ids[count] = kblocks
        ids[count + 1] = kblocks
        steps = jnp.maximum((count + 1) // 2, 1)

        def attend(steps):
            masks = [bias[ids[n]] for n in range(2 * steps)]
            rows_of = [
                pl.ds(pl.multiple_of(jnp.minimum(ids[n], kblocks - 1) * BLK, BLK), BLK)
                for n in range(2 * steps)
            ]

            def scores(p):
                cols = slice(p * LANES, (p + 1) * LANES)
                if first:
                    m = None
                else:
                    old = mx_ref[q_rows, cols]
                    turned = pltpu.roll(old, HD, 1)
                    m = jnp.concatenate([jnp.where(low, old, turned), jnp.where(low, turned, old)], 0)
                q = jnp.concatenate([q_ref[q_rows, cols], q_ref[q_rows_high, cols]], axis=0)
                for n in range(steps):
                    k = jnp.concatenate(
                        [k_all[rows_of[2 * n], cols], k_all[rows_of[2 * n + 1], cols]], axis=0
                    )
                    s = lax.dot_general(
                        q, k, (((1,), (1,)), ((), ())), preferred_element_type=F32
                    )
                    mask = jnp.concatenate([masks[2 * n], masks[2 * n + 1]], axis=1)
                    s = s + jnp.concatenate([mask, mask], axis=0)
                    s_buf[p, n] = s
                    top = jnp.maximum(s[:, :LANES], s[:, LANES:])
                    m = top if m is None else jnp.maximum(m, top)
                m_buf[p] = jnp.broadcast_to(jnp.max(m, axis=1, keepdims=True), (2 * BLK, LANES))

            def sums(p):
                cols = slice(p * LANES, (p + 1) * LANES)
                m = m_buf[p]
                m2 = jnp.concatenate([m, m], axis=1)
                e = jnp.concatenate(
                    [jnp.exp2(s_buf[p, n] - m2).astype(BF16) for n in range(steps)], axis=1
                )
                v = jnp.concatenate([v_all[here, cols] for here in rows_of], axis=0)
                v = jnp.concatenate([v, jnp.ones_like(v)], axis=1)
                y = dot(e, v)
                o = jnp.where(low, y[:BLK, :LANES], y[BLK:, :LANES])
                l = jnp.where(low, y[:BLK, LANES:], y[BLK:, LANES:])
                m = jnp.where(low, m[:BLK], m[BLK:])
                if first:
                    o_ref[q_rows, cols] = o
                    l_ref[q_rows, cols] = l
                    mx_ref[q_rows, cols] = m
                else:
                    scale = jnp.exp2(mx_ref[q_rows, cols] - m)
                    o = o + o_ref[q_rows, cols] * scale
                    l = l + l_ref[q_rows, cols] * scale
                    a_rows = pl.ds(pl.multiple_of(t * BLK, BLK), BLK)
                    a_ref[a_rows, cols] = (o / l).astype(BF16)

            scores(0)
            for p in range(pairs):
                if p + 1 < pairs:
                    scores(p + 1)
                sums(p)

        for n in range(1, kblocks // 2 + 1):

            @pl.when(steps == n)
            def _(n=n):
                attend(n)

        return carry

    lax.fori_loop(0, blocks, one_block, 0)
    if not first:
        here = pl.ds(pl.multiple_of(q_base * BLK, BLK), blocks * BLK)
        y = dot(a_ref[...], wo[...]) + dot(g_ref[here, :], wco[...])
        out_ref[...] = y.astype(out_ref.dtype)


def attention(stage, context, queries, kv, new=(), weights=(), finish=(), columns=0, rim=0):
    rows, cols = queries.shape[0] // 2, queries.shape[1]
    pairs = cols // LANES
    keys = kv[0].shape[0] + sum(part.shape[0] for part in new)
    kblocks = keys // BLK
    steps = (kblocks + 1) // 2
    held = jax.ShapeDtypeStruct((keys, cols), BF16)
    more = []
    if stage == 0:
        out_shape = [jax.ShapeDtypeStruct((rows, cols), F32)] * 3
        out_shape += [jax.ShapeDtypeStruct((KTAP, rim), BF16)]
        kept = [pltpu.VMEM(held.shape, BF16)] * 2
    else:
        kept, more = [], [pltpu.VMEM((rows // 2, cols), BF16)]
        wide = finish[4].shape[1]
        out_shape = [jax.ShapeDtypeStruct((rows // 2, wide), BF16 if stage == 1 else F32)]
        if stage == 1:
            out_shape += [held] * 2
    operands = (queries, *kv, *new, *weights, *finish)
    here = rows if stage == 0 else rows // 2
    return pl.pallas_call(
        functools.partial(
            attention_kernel, stage, columns, len(new), context[0].shape[0], rows // BLK, kblocks
        ),
        out_shape=out_shape,
        in_specs=[SMEM] * len(context) + [VMEM] * len(operands),
        out_specs=[VMEM] * len(out_shape),
        scratch_shapes=kept
        + [
            pltpu.VMEM((pairs, steps, 2 * BLK, 2 * BLK), F32),
            pltpu.VMEM((pairs, 2 * BLK, LANES), F32),
            pltpu.VMEM((kblocks + 1, BLK, LANES), F32),
            pltpu.VMEM((kblocks, LANES), jnp.int32),
            pltpu.VMEM((BLK, LANES), jnp.int32),
            pltpu.SMEM((kblocks,), jnp.int32),
            pltpu.SMEM((kblocks + 1,), jnp.int32),
            pltpu.SMEM((kblocks + 2,), jnp.int32),
            pltpu.SMEM((4 * rows // BLK,), jnp.int32),
        ]
        + more,
        compiler_params=limit(20),
        cost_estimate=pl.CostEstimate(
            flops=4 * here * keys * cols, bytes_accessed=4 * keys * cols, transcendentals=here * keys
        ),
        name="attention",
    )(*context, *operands)


SEG = 8
KT = 8


def accumulate(accs, xv, wv):
    accs, taps = list(accs), len(wv)
    for n in range(taps):
        for j in range(len(accs)):
            accs[j] = accs[j] + xv[j - n + taps - 1] * wv[n]
    return tuple(accs)


def conv_kernel(
    nch, columns, starts, own_ref, rim_p, last, last_s, weights, taps_ref, gate_ref, out_ref, x_ref, xs, ws, ms, y, xl, tf, y2
):
    rows, cols = own_ref.shape
    span = rows // SEG
    tiles = cols // LANES
    quarter, outs = KTAP // 4, span // 4
    me = lax.axis_index("seq")
    first = me * rows

    seg = lax.broadcasted_iota(jnp.int32, (SEG, LANES), 0)
    seg_first = first + seg * span

    def latest(c, begin):
        s = starts[c]
        return jnp.where(s < seg_first + span, jnp.maximum(begin, s), begin)

    begin = lax.fori_loop(0, nch, latest, jnp.zeros((SEG, LANES), jnp.int32))
    begin = begin - seg_first
    inner = begin > 0
    outer_begin = jnp.where(inner, -(1 << 30), begin)

    wc = weights[:, columns : columns + cols]
    rim_o = dot(rim_rows((last, last_s)), wc).astype(BF16)
    for t in range(tiles):
        cols_t = slice(t * LANES, (t + 1) * LANES)
        x_ref[t, 0:KTAP, :] = jnp.where(me % 2 == 1, rim_p[:, cols_t], rim_o[:, cols_t]).astype(F32)
        x_ref[t, pl.ds(KTAP, rows), :] = own_ref[:, cols_t].astype(F32)
        x_ref[t, pl.ds(KTAP + rows, 8), :] = jnp.zeros((8, LANES), F32)

    def row_of(j, t):
        v = x_ref[t, pl.ds(KTAP + j, SEG, stride=span), :]
        return jnp.where(j >= outer_begin, v, 0.0)

    def spread(n, before):
        j = 4 * (n - (quarter - 1))
        after = []
        for t in range(tiles):
            cols_t = slice(t * LANES, (t + 1) * LANES)
            a3, a2, a1 = before[3 * t : 3 * t + 3]
            b0, b1, b2, b3 = (row_of(j + k, t) for k in range(4))
            for s, (early, here, late) in enumerate(
                ((a1 - a2, b1 - b0, b3 - b2), (a2, b0, b2), (a2 - a3, b0 - a1, b2 - b1))
            ):
                xs[3 * s, n, :, cols_t] = late - here
                xs[3 * s + 1, n, :, cols_t] = here
                xs[3 * s + 2, n, :, cols_t] = here - early
            after += [b1, b2, b3]
        return tuple(after)

    start = 4 * (1 - quarter)
    lax.fori_loop(
        0,
        quarter + outs,
        spread,
        tuple(row_of(start + k, t) for t in range(tiles) for k in (-3, -2, -1)),
        unroll=4,
    )

    def widen(g, c):
        here = pl.ds(pl.multiple_of(g * 16, 16), 16)
        w = taps_ref[here, :].astype(F32)
        for t in range(tiles):
            tf[t, here, :] = w[:, t * LANES : (t + 1) * LANES]
        for r in range(4):
            w0, w1, w2, w3 = (w[4 * r + k : 4 * r + k + 1, :] for k in range(4))
            for s, (u, v) in enumerate(((w0, w2), (w0 + w1, w2 + w3), (w1, w3))):
                for k, value in enumerate((u, u + v, v)):
                    ws[3 * s + k, 4 * g + r] = jnp.broadcast_to(value, (SEG, cols))
        return c

    lax.fori_loop(0, KTAP // 16, widen, 0)

    for t in range(tiles):
        cols_t = slice(t * LANES, (t + 1) * LANES)

        def filtered(f, c, cols_t=cols_t):
            accs = tuple(jnp.zeros((SEG, LANES), F32) for _ in range(outs))
            for k0 in range(0, quarter, KT):
                at = quarter - k0 - KT
                xv = [xs[f, at + n, :, cols_t] for n in range(outs + KT - 1)]
                wv = [ws[f, k0 + n, :, cols_t] for n in range(KT)]
                accs = accumulate(accs, xv, wv)
            for j in range(outs):
                ms[f, j] = accs[j]
            return c

        lax.fori_loop(0, 9, filtered, 0)

        def join(b, c, cols_t=cols_t):
            odd, even = [], []
            for s in range(3):
                m0, m1, m2 = (ms[3 * s + k, b] for k in range(3))
                odd.append(m0 + m1)
                even.append(m1 - m2)
            for k, (m0, m1, m2) in enumerate((even, odd)):
                y[4 * b + 2 * k + 1, :, cols_t] = m0 + m1
                y[4 * b + 2 * k, :, cols_t] = m1 - m2
            return c

        lax.fori_loop(0, outs, join, 0, unroll=4)

    def collect(j, c):
        for t in range(tiles):
            cols_t = slice(t * LANES, (t + 1) * LANES)
            y2[t, pl.ds(j, SEG, stride=span), :] = y[j, :, cols_t]
        return c

    lax.fori_loop(0, span, collect, 0, unroll=4)

    eighth = span // SEG
    xl[:, 0:span, :] = jnp.zeros((tiles, span, LANES), F32)
    row_in = lax.broadcasted_iota(jnp.int32, (span, LANES), 0)

    def repair(c, carry):
        at = starts[c] - first
        seg_at, from_row = at // span, lax.rem(at, span)

        @pl.when((at > 0) & (at < rows) & (from_row > 0))
        def _():
            base = pl.multiple_of(seg_at * span, span)
            for t in range(tiles):
                x = x_ref[t, pl.ds(KTAP + base, span), :]
                xl[t, span:, :] = jnp.where(row_in >= from_row, x, 0.0)
            for t in range(tiles):

                def taps(g, accs, t=t):
                    k0 = pl.multiple_of(g * KT, KT)
                    lo = span - k0 - (KT - 1)
                    xv = [
                        xl[t, pl.ds(lo + n, SEG, stride=eighth), :] for n in range(eighth + KT - 1)
                    ]
                    w = tf[t, pl.ds(k0, KT), :]
                    wv = [jnp.broadcast_to(w[n : n + 1, :], (SEG, LANES)) for n in range(KT)]
                    return accumulate(accs, xv, wv)

                accs = lax.fori_loop(
                    0,
                    (span - from_row + KT - 1) // KT,
                    taps,
                    tuple(jnp.zeros((SEG, LANES), F32) for _ in range(eighth)),
                )
                part = lax.broadcasted_iota(jnp.int32, (SEG, LANES), 0) * eighth
                for j in range(eighth):
                    here = pl.ds(base + j, SEG, stride=eighth)
                    y2[t, here, :] = jnp.where(part + j >= from_row, accs[j], y2[t, here, :])

        return carry

    lax.fori_loop(0, nch, repair, 0)

    def gating(r, c):
        at = pl.ds(pl.multiple_of(r * 64, 64), 64)
        for t in range(tiles):
            cols_t = slice(t * LANES, (t + 1) * LANES)
            g = gate_ref[at, cols_t].astype(F32)
            out_ref[at, cols_t] = (y2[t, at, :] * (g / (1.0 + jnp.exp(-g)))).astype(BF16)
        return c

    lax.fori_loop(0, rows // 64, gating, 0)


def convolution(columns, starts, own, rim_p, last, last_s, weights, taps, gate):
    rows, cols = own.shape
    span = rows // SEG
    quarter, outs = KTAP // 4, span // 4
    tiles = cols // LANES
    return pl.pallas_call(
        functools.partial(conv_kernel, starts.shape[0], columns),
        out_shape=jax.ShapeDtypeStruct((rows, cols), BF16),
        in_specs=[SMEM] + [VMEM] * 7,
        out_specs=VMEM,
        scratch_shapes=[
            pltpu.VMEM((tiles, KTAP + rows + 8, LANES), F32),
            pltpu.VMEM((9, quarter + outs, SEG, cols), F32),
            pltpu.VMEM((9, quarter, SEG, cols), F32),
            pltpu.VMEM((9, outs, SEG, LANES), F32),
            pltpu.VMEM((span, SEG, cols), F32),
            pltpu.VMEM((tiles, 2 * span, LANES), F32),
            pltpu.VMEM((tiles, KTAP, LANES), F32),
            pltpu.VMEM((tiles, rows, LANES), F32),
        ],
        compiler_params=limit(20),
        cost_estimate=pl.CostEstimate(
            flops=40 * rows * cols * KTAP, bytes_accessed=8 * rows * cols, transcendentals=rows * cols
        ),
    )(starts, own, rim_p, last, last_s, weights, taps, gate)


def body(
    tokens,
    norm_gain,
    w_query,
    w_key,
    w_value,
    w_out,
    conv_in_w,
    conv_gate_w,
    conv_taps,
    conv_out_w,
    chain_starts,
    block_lists,
    block_counts,
):
    shards = lax.axis_size("seq")

    after = lax.optimization_barrier
    head_cols, channels = w_query.shape[1], conv_in_w.shape[1]
    kv_columns, conv_columns = head_cols, 3 * head_cols
    mine, yours, normed, half, weights = plan(
        block_lists, tokens, norm_gain, (w_query, w_key, w_value, conv_in_w, conv_gate_w)
    )
    to_asking = flat_pairs(shards, lambda i, h: i + (-2 if h == 0 else 2))
    to_asked = flat_pairs(shards, lambda i, h: i + (2 if h == 0 else -2))
    to_partner = flat_pairs(shards, lambda i, h: i ^ 1)
    to_other = flat_pairs(shards, lambda i, h: i + (2 if i % 2 == 0 else -2))
    chunks = [half[:BLK], half[BLK:]]
    partner, other = [None] * 2, [None] * 2
    for n in range(2):
        partner[n] = lax.ppermute(chunks[n], AXES, to_partner)
    asked = lax.ppermute(mine, AXES, to_asked)

    scale = math.log2(math.e) / math.sqrt(HD)
    queries, k_own, v_own = own_project(normed, weights, 0, (head_cols,) * 3, scale)
    asked, k_own = after((asked, k_own))
    picked = pick(asked, (normed,))
    far = lax.ppermute(picked, AXES, to_asking)
    conv_input, conv_gate = own_project(normed, weights, conv_columns, (channels,) * 2)
    for n in range(2):
        other[n] = lax.ppermute(partner[n], AXES, to_other)
    partner += [swap(part) for part in partner]

    context = (chain_starts, block_lists, block_counts, mine, yours)
    *state, rim_p = attention(
        0,
        context,
        queries,
        (k_own, v_own),
        partner,
        (weights,),
        columns=kv_columns,
        rim=channels,
    )
    other, state = after((other, state))
    other += [swap(part) for part in other]
    farther = lax.ppermute(pick(asked, (*partner, *other)), AXES, to_asking)

    gated = convolution(
        conv_columns,
        chain_starts,
        conv_input,
        rim_p,
        other[1],
        other[3],
        weights,
        conv_taps,
        conv_gate,
    )
    far, farther, gated, other = after((far, farther, gated, other))
    far_s = swap(far)
    farther_s = swap(farther)
    k_o, v_o = other_project(other, weights, kv_columns, head_cols)
    finish = (*state, gated, w_out, conv_out_w)
    theirs, k_rest, v_rest = attention(
        1,
        context,
        queries,
        (k_o, v_o),
        (far, far_s, farther, farther_s),
        (weights,),
        finish,
        kv_columns,
    )
    theirs = swap(theirs)
    (ours,) = attention(2, context, queries, (k_rest, v_rest), finish=finish)
    return (ours + theirs.astype(F32)).astype(BF16)


def solution(mesh):
    return jax.shard_map(
        body,
        mesh=mesh,
        in_specs=(
            P("seq", None),
            P(),
            P(None, "head"),
            P(None, "head"),
            P(None, "head"),
            P("head", None),
            P(None, "head"),
            P(None, "head"),
            P(None, "head"),
            P("head", None),
            P(),
            P("seq", None),
            P("seq"),
        ),
        out_specs=P(("seq", "head"), None),
        check_vma=False,
    )
```

```python
import functools
import math

import jax
import jax.numpy as jnp
from jax import lax
from jax.experimental import pallas as pl
from jax.experimental.pallas import tpu as pltpu
from jax.sharding import PartitionSpec as P


HD = 64
KTAP = 128
BLK = 128
HALF = 512
NB = 4
LANES = 128
AXES = ("seq", "head")
NEG = -1e30
F32 = jnp.float32
BF16 = jnp.bfloat16


def flat_pairs(count, target):
    pairs = []
    for i in range(count):
        for h in range(2):
            j = target(i, h)
            if 0 <= j < count:
                pairs.append((2 * i + h, 2 * j + h))
    return pairs


def swap(value):
    return lax.ppermute(value, "head", [(0, 1), (1, 0)])


def dot(a, b):
    return jnp.dot(a, b, preferred_element_type=F32)


SMEM = pl.BlockSpec(memory_space=pltpu.SMEM)
VMEM = pl.BlockSpec(memory_space=pltpu.VMEM)
ANY = pl.BlockSpec(memory_space=pl.ANY)


def limit(mib):
    return pltpu.CompilerParams(vmem_limit_bytes=mib << 20)


def in_hbm(value):
    return pltpu.with_memory_space_constraint(value, pltpu.HBM)


PIECES = 4


def plan_kernel(per_shard, nweights, lists_in, counts_in, tokens, gain_in, *refs):
    weights, refs = refs[:nweights], refs[nweights:]
    mine, yours, normed, half, *refs = refs
    every, lists, counts, gain, rows, sem = refs
    kept, column = [], 0
    for w in weights:
        kept.append(every.at[:, pl.ds(column, w.shape[1])])
        column += w.shape[1]
    me, core = lax.axis_index("seq"), lax.axis_index("head")
    size = tokens.shape[0] // PIECES
    small = [
        pltpu.make_async_copy(lists_in, lists, sem.at[PIECES]),
        pltpu.make_async_copy(gain_in, gain, sem.at[PIECES + 1]),
        pltpu.make_async_copy(counts_in, counts, sem.at[PIECES + 2]),
    ]
    copies = [
        pltpu.make_async_copy(
            tokens.at[pl.ds(n * size, size)], rows.at[pl.ds(n * size, size)], sem.at[n]
        )
        for n in range(PIECES)
    ]
    copies += [
        pltpu.make_async_copy(weights[n], kept[n], sem.at[PIECES + 3 + n]) for n in range(nweights)
    ]
    for copy in small + copies:
        copy.start()
    for copy in small:
        copy.wait()
    g = jnp.broadcast_to(gain[...].reshape(1, -1), (32, normed.shape[1]))

    def norm(r, c):
        here = pl.ds(pl.multiple_of(r * 32, 32), 32)
        x = rows[here, :].astype(F32)
        x = x * lax.rsqrt(jnp.mean(x * x, axis=1, keepdims=True) + 1e-05) * g
        normed[here, :] = x.astype(BF16)
        return c

    for n in range(PIECES):
        copies[n].wait()
        lax.fori_loop(n * size // 32, (n + 1) * size // 32, norm, 0)

    def wanted(distance):
        low = (me + distance) * per_shard
        found = jnp.int32(0)
        for q in range(per_shard):
            for m in range(NB):
                local = lists[q, m] - low
                named = (local >= 0) & (local < per_shard) & (m < counts[q])
                found = jnp.where(named, local, found)
        return found

    side = 1 - 2 * core
    for n in range(2):
        mine[n] = wanted(side * (n + 2))
        yours[n] = wanted(-side * (n + 2))
    count = half.shape[0]
    half[...] = normed[pl.ds(pl.multiple_of(core * count, count), count), :]
    for copy in copies[PIECES:]:
        copy.wait()


def plan(lists, counts, tokens, gain, weights):
    rows, cols = tokens.shape
    pair = jax.ShapeDtypeStruct((2,), jnp.int32)
    return pl.pallas_call(
        functools.partial(plan_kernel, rows // BLK, len(weights)),
        out_shape=[
            pair,
            pair,
            jax.ShapeDtypeStruct((rows, cols), BF16),
            jax.ShapeDtypeStruct((rows // 2, cols), BF16),
        ]
        + [jax.ShapeDtypeStruct((cols, sum(w.shape[1] for w in weights)), BF16)],
        in_specs=[ANY] * (4 + len(weights)),
        out_specs=[SMEM, SMEM] + [VMEM] * 3,
        scratch_shapes=[
            pltpu.SMEM(lists.shape, jnp.int32),
            pltpu.SMEM(counts.shape, jnp.int32),
            pltpu.VMEM(gain.shape, F32),
            pltpu.VMEM((rows, cols), BF16),
            pltpu.SemaphoreType.DMA((PIECES + 3 + len(weights),)),
        ],
        compiler_params=limit(14),
        name="plan",
    )(in_hbm(lists), in_hbm(counts), in_hbm(tokens), in_hbm(gain), *[in_hbm(w) for w in weights])


def pick_own_kernel(asked, own, out):
    out[...] = own[pl.ds(pl.multiple_of(asked[0] * BLK, BLK), BLK), :]


def pick_other_kernel(asked, *refs):
    *parts, out = refs
    me, core = lax.axis_index("seq"), lax.axis_index("head")
    count = len(parts) // 2
    blocks = parts[0].shape[0] // BLK
    use_partner = (me % 2) == core
    slot = (asked[1] + core * (count * blocks // 2)) % (count * blocks)
    held = slot // blocks + jnp.where(use_partner, 0, count)
    here = pl.ds(pl.multiple_of((slot % blocks) * BLK, BLK), BLK)
    for k, ref in enumerate(parts):

        @pl.when(held == k)
        def _(ref=ref):
            out[...] = ref[here, :]


def pick(asked, sources):
    if len(sources) == 1:
        kernel = pick_own_kernel
    else:
        kernel = pick_other_kernel
    return pl.pallas_call(
        kernel,
        out_shape=jax.ShapeDtypeStruct((BLK, sources[0].shape[1]), BF16),
        in_specs=[SMEM] + [VMEM] * len(sources),
        out_specs=VMEM,
        compiler_params=limit(6),
        name="pick",
    )(asked, *sources)


def rim_rows(parts):
    mine, swapped = parts[len(parts) // 2 - 1], parts[-1]
    last = slice(mine.shape[0] - KTAP, mine.shape[0])
    return jnp.where(lax.axis_index("head") == 1, mine[last, :], swapped[last, :])


WIDE = 2 * LANES


def products(x, weights, columns, outs):
    where = []
    for width, store in outs:
        where += [(store, c) for c in range(0, width, LANES)]
    total = len(where) * LANES
    for n in range(0, total, WIDE):
        last = min(n + WIDE, total)
        y = dot(x, weights[:, columns + n : columns + last])
        for c in range(n, last, LANES):
            store, column = where[c // LANES]
            store(slice(column, column + LANES), y[:, c - n : c - n + LANES])


def stored_in(ref, rows=slice(None)):
    def store(cols, y):
        ref[rows, cols] = y.astype(BF16)

    return ref.shape[1], store


def own_kernel(columns, scale, x_ref, weights, *outs):
    targets = [stored_in(out) for out in outs]
    if scale is not None:
        q_ref, rows = outs[0], x_ref.shape[0]
        low = lax.broadcasted_iota(jnp.int32, (rows, LANES), 1) < HD

        def store(cols, y):
            y = (y * scale).astype(BF16)
            q_ref[:rows, cols] = jnp.where(low, y, jnp.zeros_like(y))
            q_ref[rows:, cols] = jnp.where(low, jnp.zeros_like(y), y)

        targets[0] = (q_ref.shape[1], store)
    products(x_ref[...], weights, columns, targets)


def own_project(x, weights, columns, widths, scale=None):
    rows, cols = x.shape
    outs = [jax.ShapeDtypeStruct((rows, width), BF16) for width in widths]
    if scale is not None:
        outs[0] = jax.ShapeDtypeStruct((2 * rows, widths[0]), BF16)
    return pl.pallas_call(
        functools.partial(own_kernel, columns, scale),
        out_shape=outs,
        in_specs=[VMEM] * 2,
        out_specs=[VMEM] * len(outs),
        compiler_params=limit(16),
        cost_estimate=pl.CostEstimate(
            flops=2 * rows * cols * sum(widths), bytes_accessed=2 * cols * sum(widths), transcendentals=0
        ),
        name="own_project",
    )(x, weights)


def other_kernel(columns, *refs):
    *parts, weights, k_ref, v_ref = refs
    x = jnp.concatenate([part[...] for part in parts], axis=0)
    products(x, weights, columns, [stored_in(k_ref), stored_in(v_ref)])


def other_project(parts, weights, columns, width):
    rows, cols = sum(part.shape[0] for part in parts), parts[0].shape[1]
    return pl.pallas_call(
        functools.partial(other_kernel, columns),
        out_shape=[jax.ShapeDtypeStruct((rows, width), BF16)] * 2,
        in_specs=[VMEM] * (1 + len(parts)),
        out_specs=[VMEM] * 2,
        compiler_params=limit(14),
        cost_estimate=pl.CostEstimate(
            flops=4 * rows * cols * width, bytes_accessed=4 * cols * width, transcendentals=0
        ),
        name="other_project",
    )(*parts, weights)


BIG = 1 << 30
FAR = 1 << 20


def attention_kernel(
    stage,
    columns,
    fresh_parts,
    nch,
    per_shard,
    kblocks,
    starts,
    lists,
    counts,
    mine,
    yours,
    q_ref,
    k_in,
    v_in,
    *refs,
):
    first = stage == 0
    new, refs = refs[:fresh_parts], refs[fresh_parts:]
    if stage < 2:
        weights, *refs = refs
    if first:
        o_ref, l_ref, mx_ref, rim_ref, k_all, v_all, *refs = refs
    else:
        o_ref, l_ref, mx_ref, g_ref, wo, wco, out_ref, *refs = refs
        k_all, v_all, refs = (refs[0], refs[1], refs[2:]) if stage == 1 else (k_in, v_in, refs)
    s_buf, m_buf, bias, k_chain, i_chain, gblk, flag, ids, around, *refs = refs
    a_ref = None if first else refs[0]
    pairs = q_ref.shape[1] // LANES
    if stage < 2:
        held = k_in.shape[0]
        k_all[:held] = k_in[...]
        v_all[:held] = v_in[...]
        fresh = jnp.concatenate([part[...] for part in new], axis=0)
        rest = slice(held, None)
        products(fresh, weights, columns, [stored_in(k_all, rest), stored_in(v_all, rest)])
    if first:
        conv_columns = columns + 2 * k_in.shape[1]
        products(rim_rows(new), weights, conv_columns, [stored_in(rim_ref)])

    me, core = lax.axis_index("seq"), lax.axis_index("head")
    shards = lax.axis_size("seq")
    step = 1 - 2 * (me % 2)
    side = 1 - 2 * core
    turn = core * (per_shard // 2)
    own = me * per_shard

    def block_of(shard, local):
        return jnp.where((shard >= 0) & (shard < shards), shard * per_shard + local, -FAR)

    for p in range(per_shard):
        local = (turn + p) % per_shard
        if first:
            gblk[p] = own + p
            gblk[per_shard + p] = block_of(me + step, local)
        else:
            gblk[p] = block_of(me - step, local)
    if not first:
        for n in range(2):
            gblk[per_shard + 2 * n] = block_of(me + side * (n + 2), mine[n])
            gblk[per_shard + 2 * n + 1] = block_of(me - side * (n + 2), yours[n])

    def slot_of(block):
        shard = block // per_shard
        away = shard - me
        near_slot = (block % per_shard - turn) % per_shard
        if first:
            return jnp.where(away == step, per_shard + near_slot, kblocks)
        far_slot = per_shard + 2 * (jnp.abs(away) - 2) + jnp.where(away * side > 0, 0, 1)
        return jnp.where(
            away == -step, near_slot, jnp.where(jnp.abs(away) >= 2, far_slot, kblocks)
        )

    def chain_of(pos):
        return lax.fori_loop(
            0,
            nch,
            lambda c, n: n + jnp.where(starts[c] <= pos, 1, 0),
            jnp.full(pos.shape, -1, jnp.int32),
        )

    lane = lax.broadcasted_iota(jnp.int32, (BLK, LANES), 1)
    row = lax.broadcasted_iota(jnp.int32, (BLK, LANES), 0)
    low = lane < HD
    for b in range(kblocks):
        k_chain[pl.ds(b, 1), :] = gblk[b] * BLK + lane[0:1, :]
    k_chain[...] = chain_of(k_chain[...])
    bias[kblocks] = jnp.full((BLK, LANES), NEG, F32)

    def scan(c, found):
        s, out = starts[c], []
        for n in range(per_shard):
            q_first = (own + n) * BLK
            chain, begin, end, after = found[4 * n : 4 * n + 4]
            ahead = s <= q_first
            out += [
                chain + ahead.astype(jnp.int32),
                jnp.where(ahead, jnp.maximum(begin, s), begin),
                jnp.where(ahead, end, jnp.minimum(end, s)),
                jnp.where(s > q_first + BLK - 1, jnp.minimum(after, s), after),
            ]
        return tuple(out)

    none = (jnp.int32(-1), jnp.int32(0), jnp.int32(BIG), jnp.int32(BIG))
    for n, value in enumerate(lax.fori_loop(0, nch, scan, none * per_shard)):
        around[n] = value

    blocks = per_shard if first else per_shard // 2
    q_base = (0, (1 - core) * blocks, core * blocks)[stage]

    def one_block(t, carry):
        qb = q_base + t
        gq = own + qb
        q_first = gq * BLK
        q_last = q_first + BLK - 1
        chain, begin, end, after = (around[4 * qb + n] for n in range(4))
        i_chain[...] = jnp.where(q_first + row >= end, chain + 1, chain)
        q_rows = pl.ds(pl.multiple_of(qb * BLK, BLK), BLK)
        q_rows_high = pl.ds(pl.multiple_of((per_shard + qb) * BLK, BLK), BLK)

        for b in range(kblocks + 1):
            flag[b] = 0

        def mark(m, c):
            flag[slot_of(lists[qb, m])] = 1
            return c

        lax.fori_loop(0, counts[qb], mark, 0)

        count = jnp.int32(0)
        for b in range(kblocks):
            gk = gblk[b]
            k_first = gk * BLK
            k_last = k_first + BLK - 1
            away = gk - gq
            near = (jnp.abs(away) * BLK <= HALF) & (k_last >= begin) & (k_first < after)
            listed = flag[b]
            one_chain = (k_first >= begin) & (jnp.maximum(k_last, q_last) < end)
            active = near | ((listed == 1) & jnp.logical_not(one_chain))
            ids[count] = b
            count = count + active.astype(jnp.int32)
            same = i_chain[...] == k_chain[b : b + 1, :]
            if first and b < per_shard:
                bias[b] = jnp.where(same, 0.0, NEG)
                continue
            relative = away * BLK + lane - row
            in_window = jnp.where((relative >= -HALF) & (relative < HALF), 0.0, NEG)
            in_list = jnp.where(listed == 1, 0.0, NEG)
            bias[b] = jnp.where(same, in_window, in_list)
        ids[count] = kblocks
        ids[count + 1] = kblocks
        steps = jnp.maximum((count + 1) // 2, 1)

        def attend(steps):
            masks = [bias[ids[n]] for n in range(2 * steps)]
            rows_of = [
                pl.ds(pl.multiple_of(jnp.minimum(ids[n], kblocks - 1) * BLK, BLK), BLK)
                for n in range(2 * steps)
            ]

            def scores(p):
                cols = slice(p * LANES, (p + 1) * LANES)
                if first:
                    m = None
                else:
                    old = mx_ref[q_rows, cols]
                    turned = pltpu.roll(old, HD, 1)
                    m = jnp.concatenate([jnp.where(low, old, turned), jnp.where(low, turned, old)], 0)
                q = jnp.concatenate([q_ref[q_rows, cols], q_ref[q_rows_high, cols]], axis=0)
                for n in range(steps):
                    k = jnp.concatenate(
                        [k_all[rows_of[2 * n], cols], k_all[rows_of[2 * n + 1], cols]], axis=0
                    )
                    s = lax.dot_general(
                        q, k, (((1,), (1,)), ((), ())), preferred_element_type=F32
                    )
                    mask = jnp.concatenate([masks[2 * n], masks[2 * n + 1]], axis=1)
                    s = s + jnp.concatenate([mask, mask], axis=0)
                    s_buf[p, n] = s
                    top = jnp.maximum(s[:, :LANES], s[:, LANES:])
                    m = top if m is None else jnp.maximum(m, top)
                m_buf[p] = jnp.broadcast_to(jnp.max(m, axis=1, keepdims=True), (2 * BLK, LANES))

            def sums(p):
                cols = slice(p * LANES, (p + 1) * LANES)
                m = m_buf[p]
                m2 = jnp.concatenate([m, m], axis=1)
                e = jnp.concatenate(
                    [jnp.exp2(s_buf[p, n] - m2).astype(BF16) for n in range(steps)], axis=1
                )
                v = jnp.concatenate([v_all[here, cols] for here in rows_of], axis=0)
                v = jnp.concatenate([v, jnp.ones_like(v)], axis=1)
                y = dot(e, v)
                o = jnp.where(low, y[:BLK, :LANES], y[BLK:, :LANES])
                l = jnp.where(low, y[:BLK, LANES:], y[BLK:, LANES:])
                m = jnp.where(low, m[:BLK], m[BLK:])
                if first:
                    o_ref[q_rows, cols] = o
                    l_ref[q_rows, cols] = l
                    mx_ref[q_rows, cols] = m
                else:
                    scale = jnp.exp2(mx_ref[q_rows, cols] - m)
                    o = o + o_ref[q_rows, cols] * scale
                    l = l + l_ref[q_rows, cols] * scale
                    a_rows = pl.ds(pl.multiple_of(t * BLK, BLK), BLK)
                    a_ref[a_rows, cols] = (o / l).astype(BF16)

            scores(0)
            for p in range(pairs):
                if p + 1 < pairs:
                    scores(p + 1)
                sums(p)

        for n in range(1, kblocks // 2 + 1):

            @pl.when(steps == n)
            def _(n=n):
                attend(n)

        return carry

    lax.fori_loop(0, blocks, one_block, 0)
    if not first:
        here = pl.ds(pl.multiple_of(q_base * BLK, BLK), blocks * BLK)
        y = dot(a_ref[...], wo[...]) + dot(g_ref[here, :], wco[...])
        out_ref[...] = y.astype(out_ref.dtype)


def attention(stage, context, queries, kv, new=(), weights=(), finish=(), columns=0, rim=0):
    rows, cols = queries.shape[0] // 2, queries.shape[1]
    pairs = cols // LANES
    keys = kv[0].shape[0] + sum(part.shape[0] for part in new)
    kblocks = keys // BLK
    steps = (kblocks + 1) // 2
    held = jax.ShapeDtypeStruct((keys, cols), BF16)
    more = []
    if stage == 0:
        out_shape = [jax.ShapeDtypeStruct((rows, cols), F32)] * 3
        out_shape += [jax.ShapeDtypeStruct((KTAP, rim), BF16)]
        kept = [pltpu.VMEM(held.shape, BF16)] * 2
    else:
        kept, more = [], [pltpu.VMEM((rows // 2, cols), BF16)]
        wide = finish[4].shape[1]
        out_shape = [jax.ShapeDtypeStruct((rows // 2, wide), BF16 if stage == 1 else F32)]
        if stage == 1:
            out_shape += [held] * 2
    operands = (queries, *kv, *new, *weights, *finish)
    here = rows if stage == 0 else rows // 2
    return pl.pallas_call(
        functools.partial(
            attention_kernel, stage, columns, len(new), context[0].shape[0], rows // BLK, kblocks
        ),
        out_shape=out_shape,
        in_specs=[SMEM] * len(context) + [VMEM] * len(operands),
        out_specs=[VMEM] * len(out_shape),
        scratch_shapes=kept
        + [
            pltpu.VMEM((pairs, steps, 2 * BLK, 2 * BLK), F32),
            pltpu.VMEM((pairs, 2 * BLK, LANES), F32),
            pltpu.VMEM((kblocks + 1, BLK, LANES), F32),
            pltpu.VMEM((kblocks, LANES), jnp.int32),
            pltpu.VMEM((BLK, LANES), jnp.int32),
            pltpu.SMEM((kblocks,), jnp.int32),
            pltpu.SMEM((kblocks + 1,), jnp.int32),
            pltpu.SMEM((kblocks + 2,), jnp.int32),
            pltpu.SMEM((4 * rows // BLK,), jnp.int32),
        ]
        + more,
        compiler_params=limit(20),
        cost_estimate=pl.CostEstimate(
            flops=4 * here * keys * cols, bytes_accessed=4 * keys * cols, transcendentals=here * keys
        ),
        name="attention",
    )(*context, *operands)


SEG = 8
KT = 8


def accumulate(accs, xv, wv):
    accs, taps = list(accs), len(wv)
    for n in range(taps):
        for j in range(len(accs)):
            accs[j] = accs[j] + xv[j - n + taps - 1] * wv[n]
    return tuple(accs)


def conv_kernel(
    nch, columns, starts, own_ref, rim_p, last, last_s, weights, taps_ref, gate_ref, out_ref, x_ref, xs, ws, ms, y, xl, tf, y2
):
    rows, cols = own_ref.shape
    span = rows // SEG
    tiles = cols // LANES
    quarter, outs = KTAP // 4, span // 4
    me = lax.axis_index("seq")
    first = me * rows

    seg = lax.broadcasted_iota(jnp.int32, (SEG, LANES), 0)
    seg_first = first + seg * span

    def latest(c, begin):
        s = starts[c]
        return jnp.where(s < seg_first + span, jnp.maximum(begin, s), begin)

    begin = lax.fori_loop(0, nch, latest, jnp.zeros((SEG, LANES), jnp.int32))
    begin = begin - seg_first
    inner = begin > 0
    outer_begin = jnp.where(inner, -(1 << 30), begin)

    wc = weights[:, columns : columns + cols]
    rim_o = dot(rim_rows((last, last_s)), wc).astype(BF16)
    for t in range(tiles):
        cols_t = slice(t * LANES, (t + 1) * LANES)
        x_ref[t, 0:KTAP, :] = jnp.where(me % 2 == 1, rim_p[:, cols_t], rim_o[:, cols_t]).astype(F32)
        x_ref[t, pl.ds(KTAP, rows), :] = own_ref[:, cols_t].astype(F32)
        x_ref[t, pl.ds(KTAP + rows, 8), :] = jnp.zeros((8, LANES), F32)

    def row_of(j, t):
        v = x_ref[t, pl.ds(KTAP + j, SEG, stride=span), :]
        return jnp.where(j >= outer_begin, v, 0.0)

    def spread(n, before):
        j = 4 * (n - (quarter - 1))
        after = []
        for t in range(tiles):
            cols_t = slice(t * LANES, (t + 1) * LANES)
            a3, a2, a1 = before[3 * t : 3 * t + 3]
            b0, b1, b2, b3 = (row_of(j + k, t) for k in range(4))
            for s, (early, here, late) in enumerate(
                ((a1 - a2, b1 - b0, b3 - b2), (a2, b0, b2), (a2 - a3, b0 - a1, b2 - b1))
            ):
                xs[3 * s, n, :, cols_t] = late - here
                xs[3 * s + 1, n, :, cols_t] = here
                xs[3 * s + 2, n, :, cols_t] = here - early
            after += [b1, b2, b3]
        return tuple(after)

    start = 4 * (1 - quarter)
    lax.fori_loop(
        0,
        quarter + outs,
        spread,
        tuple(row_of(start + k, t) for t in range(tiles) for k in (-3, -2, -1)),
        unroll=4,
    )

    def widen(g, c):
        here = pl.ds(pl.multiple_of(g * 16, 16), 16)
        w = taps_ref[here, :].astype(F32)
        for t in range(tiles):
            tf[t, here, :] = w[:, t * LANES : (t + 1) * LANES]
        for r in range(4):
            w0, w1, w2, w3 = (w[4 * r + k : 4 * r + k + 1, :] for k in range(4))
            for s, (u, v) in enumerate(((w0, w2), (w0 + w1, w2 + w3), (w1, w3))):
                for k, value in enumerate((u, u + v, v)):
                    ws[3 * s + k, 4 * g + r] = jnp.broadcast_to(value, (SEG, cols))
        return c

    lax.fori_loop(0, KTAP // 16, widen, 0)

    for t in range(tiles):
        cols_t = slice(t * LANES, (t + 1) * LANES)

        def filtered(f, c, cols_t=cols_t):
            accs = tuple(jnp.zeros((SEG, LANES), F32) for _ in range(outs))
            for k0 in range(0, quarter, KT):
                at = quarter - k0 - KT
                xv = [xs[f, at + n, :, cols_t] for n in range(outs + KT - 1)]
                wv = [ws[f, k0 + n, :, cols_t] for n in range(KT)]
                accs = accumulate(accs, xv, wv)
            for j in range(outs):
                ms[f, j] = accs[j]
            return c

        lax.fori_loop(0, 9, filtered, 0)

        def join(b, c, cols_t=cols_t):
            odd, even = [], []
            for s in range(3):
                m0, m1, m2 = (ms[3 * s + k, b] for k in range(3))
                odd.append(m0 + m1)
                even.append(m1 - m2)
            for k, (m0, m1, m2) in enumerate((even, odd)):
                y[4 * b + 2 * k + 1, :, cols_t] = m0 + m1
                y[4 * b + 2 * k, :, cols_t] = m1 - m2
            return c

        lax.fori_loop(0, outs, join, 0, unroll=4)

    def collect(j, c):
        for t in range(tiles):
            cols_t = slice(t * LANES, (t + 1) * LANES)
            y2[t, pl.ds(j, SEG, stride=span), :] = y[j, :, cols_t]
        return c

    lax.fori_loop(0, span, collect, 0, unroll=4)

    eighth = span // SEG
    xl[:, 0:span, :] = jnp.zeros((tiles, span, LANES), F32)
    row_in = lax.broadcasted_iota(jnp.int32, (span, LANES), 0)

    def repair(c, carry):
        at = starts[c] - first
        seg_at, from_row = at // span, lax.rem(at, span)

        @pl.when((at > 0) & (at < rows) & (from_row > 0))
        def _():
            base = pl.multiple_of(seg_at * span, span)
            for t in range(tiles):
                x = x_ref[t, pl.ds(KTAP + base, span), :]
                xl[t, span:, :] = jnp.where(row_in >= from_row, x, 0.0)
            for t in range(tiles):

                def taps(g, accs, t=t):
                    k0 = pl.multiple_of(g * KT, KT)
                    lo = span - k0 - (KT - 1)
                    xv = [
                        xl[t, pl.ds(lo + n, SEG, stride=eighth), :] for n in range(eighth + KT - 1)
                    ]
                    w = tf[t, pl.ds(k0, KT), :]
                    wv = [jnp.broadcast_to(w[n : n + 1, :], (SEG, LANES)) for n in range(KT)]
                    return accumulate(accs, xv, wv)

                accs = lax.fori_loop(
                    0,
                    (span - from_row + KT - 1) // KT,
                    taps,
                    tuple(jnp.zeros((SEG, LANES), F32) for _ in range(eighth)),
                )
                part = lax.broadcasted_iota(jnp.int32, (SEG, LANES), 0) * eighth
                for j in range(eighth):
                    here = pl.ds(base + j, SEG, stride=eighth)
                    y2[t, here, :] = jnp.where(part + j >= from_row, accs[j], y2[t, here, :])

        return carry

    lax.fori_loop(0, nch, repair, 0)

    def gating(r, c):
        at = pl.ds(pl.multiple_of(r * 64, 64), 64)
        for t in range(tiles):
            cols_t = slice(t * LANES, (t + 1) * LANES)
            g = gate_ref[at, cols_t].astype(F32)
            out_ref[at, cols_t] = (y2[t, at, :] * (g / (1.0 + jnp.exp(-g)))).astype(BF16)
        return c

    lax.fori_loop(0, rows // 64, gating, 0)


def convolution(columns, starts, own, rim_p, last, last_s, weights, taps, gate):
    rows, cols = own.shape
    span = rows // SEG
    quarter, outs = KTAP // 4, span // 4
    tiles = cols // LANES
    return pl.pallas_call(
        functools.partial(conv_kernel, starts.shape[0], columns),
        out_shape=jax.ShapeDtypeStruct((rows, cols), BF16),
        in_specs=[SMEM] + [VMEM] * 7,
        out_specs=VMEM,
        scratch_shapes=[
            pltpu.VMEM((tiles, KTAP + rows + 8, LANES), F32),
            pltpu.VMEM((9, quarter + outs, SEG, cols), F32),
            pltpu.VMEM((9, quarter, SEG, cols), F32),
            pltpu.VMEM((9, outs, SEG, LANES), F32),
            pltpu.VMEM((span, SEG, cols), F32),
            pltpu.VMEM((tiles, 2 * span, LANES), F32),
            pltpu.VMEM((tiles, KTAP, LANES), F32),
            pltpu.VMEM((tiles, rows, LANES), F32),
        ],
        compiler_params=limit(20),
        cost_estimate=pl.CostEstimate(
            flops=40 * rows * cols * KTAP, bytes_accessed=8 * rows * cols, transcendentals=rows * cols
        ),
    )(starts, own, rim_p, last, last_s, weights, taps, gate)


def body(
    tokens,
    norm_gain,
    w_query,
    w_key,
    w_value,
    w_out,
    conv_in_w,
    conv_gate_w,
    conv_taps,
    conv_out_w,
    chain_starts,
    block_lists,
    block_counts,
):
    shards = lax.axis_size("seq")

    after = lax.optimization_barrier
    head_cols, channels = w_query.shape[1], conv_in_w.shape[1]
    kv_columns, conv_columns = head_cols, 3 * head_cols
    mine, yours, normed, half, weights = plan(
        block_lists, block_counts, tokens, norm_gain, (w_query, w_key, w_value, conv_in_w, conv_gate_w)
    )
    to_asking = flat_pairs(shards, lambda i, h: i + (-2 if h == 0 else 2))
    to_asked = flat_pairs(shards, lambda i, h: i + (2 if h == 0 else -2))
    to_partner = flat_pairs(shards, lambda i, h: i ^ 1)
    to_other = flat_pairs(shards, lambda i, h: i + (2 if i % 2 == 0 else -2))
    chunks = [half[:BLK], half[BLK:]]
    partner, other = [None] * 2, [None] * 2
    for n in range(2):
        partner[n] = lax.ppermute(chunks[n], AXES, to_partner)
    asked = lax.ppermute(mine, AXES, to_asked)

    scale = math.log2(math.e) / math.sqrt(HD)
    queries, k_own, v_own = own_project(normed, weights, 0, (head_cols,) * 3, scale)
    asked, k_own = after((asked, k_own))
    picked = pick(asked, (normed,))
    far = lax.ppermute(picked, AXES, to_asking)
    conv_input, conv_gate = own_project(normed, weights, conv_columns, (channels,) * 2)
    for n in range(2):
        other[n] = lax.ppermute(partner[n], AXES, to_other)
    partner += [swap(part) for part in partner]

    context = (chain_starts, block_lists, block_counts, mine, yours)
    *state, rim_p = attention(
        0,
        context,
        queries,
        (k_own, v_own),
        partner,
        (weights,),
        columns=kv_columns,
        rim=channels,
    )
    other, state = after((other, state))
    other += [swap(part) for part in other]
    farther = lax.ppermute(pick(asked, (*partner, *other)), AXES, to_asking)

    gated = convolution(
        conv_columns,
        chain_starts,
        conv_input,
        rim_p,
        other[1],
        other[3],
        weights,
        conv_taps,
        conv_gate,
    )
    far, farther, gated, other = after((far, farther, gated, other))
    far_s = swap(far)
    farther_s = swap(farther)
    k_o, v_o = other_project(other, weights, kv_columns, head_cols)
    finish = (*state, gated, w_out, conv_out_w)
    theirs, k_rest, v_rest = attention(
        1,
        context,
        queries,
        (k_o, v_o),
        (far, far_s, farther, farther_s),
        (weights,),
        finish,
        kv_columns,
    )
    theirs = swap(theirs)
    (ours,) = attention(2, context, queries, (k_rest, v_rest), finish=finish)
    return (ours + theirs.astype(F32)).astype(BF16)


def solution(mesh):
    return jax.shard_map(
        body,
        mesh=mesh,
        in_specs=(
            P("seq", None),
            P(),
            P(None, "head"),
            P(None, "head"),
            P(None, "head"),
            P("head", None),
            P(None, "head"),
            P(None, "head"),
            P(None, "head"),
            P("head", None),
            P(),
            P("seq", None),
            P("seq"),
        ),
        out_specs=P(("seq", "head"), None),
        check_vma=False,
    )
```
